32 devices in a mesh: worker: 8 (over z, x), tok: 4 (over y, core).
Axes of the slice: x: 2, y: 2, z: 4, core: 2. Of those that a mesh axis runs over, the one named last changes fastest.
Arguments:
- inputs: bfloat16 [8, 6144, 2048], P('worker', 'tok'), may hold values from -6 to 6
- cotangent: bfloat16 [8, 6144, 1024], P('worker', 'tok'), may hold values from -0.076171875 to 0.076171875
- weights: float32 [8, 2048, 1024], P('worker', 'tok'), may hold values from -12 to 12
- momentum: float32 [8, 2048, 1024], P('worker', 'tok'), may hold values from -6 to 6
- mix_weights: int32 [8, 5], P('worker'), may hold values from 1 to 5
- clip_radius: int32 [2], replicated, may hold values from 700 to 2299
Outputs:
- new_weights: float32 [8, 2048, 1024], P('worker', 'tok')
- new_momentum: float32 [8, 2048, 1024], P('worker', 'tok')
The draws below stay inside these ranges and needn't reach their ends.
All inputs are finite; a program needn't handle non-finite values.
Results may differ from the reference program's by a relative error of at most 0.0003.
Values sent between devices are 32-bit elements; how exact they have to be, the bound alone decides.
No kernel may reach another device: no remote copies, remote signals or barrier semaphores. Data moves between devices by JAX's collectives and lax.ppermute only.
A program may use at most 64 MiB of HBM per device.

```python
import math
import jax
import jax.numpy as jnp
from jax import lax

D = 2048
KV_WIDTH = 512
ROUNDS = 2
TOKENS = 6144
WORKERS = 8


def draw_weights(key, part):
    base_key = jax.random.fold_in(key, 11)
    scale_key, entry_key = jax.random.split(base_key, 2)
    shape = (WORKERS, D, 2 * KV_WIDTH)
    worker_scale = jnp.exp(jax.random.uniform(scale_key, (WORKERS, 1, 1), jnp.float32, jnp.log(0.25), 0.0))
    row_scale = (1.0 + 2.0 * jnp.arange(D, dtype=jnp.float32) / (D - 1)).reshape(1, D, 1)
    entries = jax.random.truncated_normal(entry_key, -4.0, 4.0, shape, jnp.float32)
    return (entries * worker_scale * row_scale).astype(jnp.float32)


def touch_ends(values, key, low, largest):
    longest = values.shape.index(max(values.shape))
    spots = []
    for shift in (0, 1):
        where = [jax.random.randint(jax.random.fold_in(key, axis), (), 0, length) for axis, length in enumerate(values.shape)]
        where[longest] = (where[longest] + shift) % values.shape[longest]
        spots.append(tuple(where))
    return values.at[spots[0]].set(low).at[spots[1]].set(largest)


def block_levels(own_key, extent, cuts, low, high):
    loudness, own = 1.0, jax.random.fold_in(own_key, 6)
    for dim, shards_of in cuts:
        steps = jnp.exp(jax.random.uniform(jax.random.fold_in(own, dim), (shards_of,), jnp.float32, low / len(cuts), high / len(cuts)))
        loudness = loudness * jnp.repeat(steps, extent[dim] // shards_of).reshape([-1 if axis == dim else 1 for axis in range(len(extent))])
    return loudness


def scatter_about(key, dims, scale, limit, pieces=(), kind=jnp.bfloat16):
    drawn = jax.random.normal(key, dims, jnp.float32) * scale
    if len(pieces) > 0:
        drawn = block_levels(key, dims, pieces, -0.22, 0.18) * drawn
    return jnp.clip(drawn, min=-limit, max=limit).astype(kind)


def setup_inputs(seed: int = 0) -> dict:
    key_of = jax.random.split(jax.random.key(seed), 7)
    return {
        "inputs": scatter_about(key_of[0], (WORKERS, TOKENS, D), 1.0, 6.0, ((0, 8), (1, 4))),
        "cotangent": scatter_about(key_of[1], (WORKERS, TOKENS, 2 * KV_WIDTH), (TOKENS ** -0.5), 0.076171875, ((0, 8), (1, 4))),
        "weights": draw_weights(jax.random.fold_in(key_of[6], 71), 0),
        "momentum": scatter_about(key_of[3], (WORKERS, D, 2 * KV_WIDTH), 1.0, 6.0, ((0, 8), (1, 4)), jnp.float32),
        "mix_weights": touch_ends(jax.random.randint(key_of[4], (WORKERS, 5), 1, 6), jax.random.fold_in(key_of[4], 1), 1, 5).astype(jnp.int32),
        "clip_radius": jax.random.randint(key_of[5], (ROUNDS,), 700, 2300).astype(jnp.int32),
    }


LEARNING_RATE = 0.25

def reference(inputs, cotangent, weights, momentum, mix_weights, clip_radius):

    def worker_gradient(pair):
        features, upstream = pair
        return lax.dot_general(features, upstream, (((0,), (0,)), ((), ())), preferred_element_type=jnp.float32)
    gradient = lax.map(worker_gradient, (inputs, cotangent))
    velocity = 0.5 * momentum + gradient
    current = weights - LEARNING_RATE * velocity
    mixing = mix_weights.astype(jnp.float32)
    shares = mixing / lax.optimization_barrier(jnp.sum(mixing, axis=1, keepdims=True))
    radius_all = clip_radius.astype(jnp.float32) * (math.sqrt(D * KV_WIDTH) / 1000.0)
    worker_ids = jnp.arange(WORKERS, dtype=jnp.int32)
    neighbour_ids = [worker_ids ^ 1, worker_ids ^ 2, (worker_ids - 4) % WORKERS, (worker_ids + 4) % WORKERS]
    for round_index in range(ROUNDS):
        radius = radius_all[round_index]
        mixed_step = jnp.zeros((WORKERS, D, 2, KV_WIDTH), jnp.float32)
        for position, peer_ids in enumerate(neighbour_ids):
            difference = current[peer_ids] - current
            halves = difference.reshape(WORKERS, D, 2, KV_WIDTH)
            distance = jnp.sqrt(lax.optimization_barrier(jnp.sum(halves * halves, axis=(1, 3))))
            factor = radius / jnp.maximum(distance, radius)
            scaled = halves * (shares[:, position + 1][:, None] * factor)[:, None, :, None]
            mixed_step = mixed_step + scaled
        current = current + mixed_step.reshape(current.shape)
    return (current, velocity)
```

```python
import math

import jax
import jax.numpy as jnp
from jax import lax
from jax.sharding import PartitionSpec as P

D = 2048
KV_WIDTH = 512
ROUNDS = 2
LEARNING_RATE = 0.25
HIGH = lax.Precision.HIGHEST


def flip(value, axis, mask):
    pairs = [(source, source ^ mask) for source in range(lax.axis_size(axis))]
    return lax.ppermute(value, axis, pairs)


def chunk_units(rows, workers):
    units = rows // (8 * workers)
    count = min(4, units)
    return [units // count * 8 * workers] * count


def neighbour_table(workers):
    table = []
    for w in range(workers):
        table.append([w ^ 1, w ^ 2, (w - 4) % workers, (w + 4) % workers])
    return table


def mixing_matrices(squares, mixing, radius_all):
    workers = squares.shape[1]
    shares = mixing / jnp.sum(mixing, axis=1, keepdims=True)
    select = jnp.zeros((workers, workers), jnp.float32)
    table = jnp.array(neighbour_table(workers), jnp.int32)
    columns = jnp.arange(workers, dtype=jnp.int32)
    for k in range(4):
        hit = (table[:, k][:, None] == columns[None, :]).astype(jnp.float32)
        select = select + hit * shares[:, k + 1][:, None]
    eye = (columns[:, None] == columns[None, :]).astype(jnp.float32)[None]
    total = jnp.broadcast_to(eye, squares.shape)
    now = squares
    for r in range(ROUNDS):
        radius = radius_all[r]
        factor = radius / jnp.maximum(jnp.sqrt(jnp.maximum(now, 0.0)), radius)
        step = select[None] * factor
        step = step + eye * (1.0 - jnp.sum(step, axis=2, keepdims=True))
        total = jnp.einsum("hij,hjk->hik", step, total, precision=HIGH)
        if r + 1 < ROUNDS:
            inner = jnp.einsum("hij,hjk->hik", total, squares, precision=HIGH)
            inner = jnp.einsum("hik,hlk->hil", inner, total, precision=HIGH)
            diag = jnp.sum(inner * eye, axis=2)
            now = inner - 0.5 * (diag[:, :, None] + diag[:, None, :])
    return total


def per_device(inputs, cotangent, weights, momentum, mix_weights, clip_radius):
    features, upstream = inputs[0], cotangent[0]
    tokens = lax.axis_size("tok")
    workers = lax.axis_size("worker")
    tok, me = lax.axis_index("tok"), lax.axis_index("worker")
    rows, width = weights.shape[1:]
    half = width // 2

    def partial_rows(offset, start, size):
        block = lax.dynamic_slice_in_dim(features, (tok ^ offset) * rows + start, size, axis=1)
        return lax.dot_general(block, upstream, (((0,), (0,)), ((), ())), preferred_element_type=jnp.float32)

    def reduced(offset, level, start, size):
        if level == 0:
            return partial_rows(offset, start, size)
        mask = 1 << (level - 1)
        away = reduced(offset ^ mask, level - 1, start, size)
        return reduced(offset, level - 1, start, size) + flip(away, "tok", mask)

    levels = tokens.bit_length() - 1
    start = 0
    velocities, gathered = [], []
    for size in chunk_units(rows, workers):
        gradient = reduced(0, levels, start, size)
        velocity = 0.5 * momentum[0, start : start + size] + gradient
        current = weights[0, start : start + size] - LEARNING_RATE * velocity
        velocities.append(velocity)
        gathered.append(
            lax.all_to_all(current.reshape(workers, size // workers, width), "worker", 0, 0, tiled=True)
        )
        start += size
    squares = jnp.zeros((2, workers, workers), jnp.float32)
    pairs = {}
    for block in gathered:
        for a in range(workers):
            for b in range(a + 1, workers):
                gap = block[a] - block[b]
                gap = jnp.sum((gap * gap).reshape(-1, 2, half), axis=(0, 2))
                pairs[a, b] = pairs[a, b] + gap if (a, b) in pairs else gap
    zero = jnp.zeros((2,), jnp.float32)
    squares = jnp.stack(
        [jnp.stack([zero if a == b else pairs[min(a, b), max(a, b)] for b in range(workers)], 1) for a in range(workers)], 1
    )
    mine = (jnp.arange(workers) == me).astype(jnp.float32)[:, None]
    mixing = mine * mix_weights.astype(jnp.float32) * (1.0 / tokens)
    packed = jnp.concatenate([squares.reshape(-1), mixing.reshape(-1)])
    packed = jnp.pad(packed, (0, -packed.size % 1024)).reshape(-1, 128)
    for axis, size in (("tok", tokens), ("worker", workers)):
        mask = 1
        while mask < size:
            packed = packed + flip(packed, axis, mask)
            mask *= 2
    packed = packed.reshape(-1)
    squares = packed[: 2 * workers * workers].reshape(2, workers, workers)
    mixing = packed[2 * workers * workers :][: workers * 5].reshape(workers, 5)
    radius_all = clip_radius.astype(jnp.float32) * (math.sqrt(D * KV_WIDTH) / 1000.0)
    matrix = mixing_matrices(squares, mixing, radius_all)
    news = []
    for block in gathered:
        mixed = []
        for w in range(workers):
            total = 0.0
            for j in range(workers):
                scale = jnp.repeat(matrix[:, w, j], half)
                total = total + block[j] * scale[None, :]
            mixed.append(total)
        news.append(jnp.stack(mixed))
    news = jnp.concatenate(news, axis=1)
    news = lax.all_to_all(news, "worker", 0, 0, tiled=True)
    out, start = [], 0
    for block in gathered:
        size = block.shape[1]
        out.append(news[:, start : start + size].reshape(-1, width))
        start += size
    return jnp.concatenate(out)[None], jnp.concatenate(velocities)[None]


def solution(mesh):
    placed = (
        P("worker", "tok", None),
        P("worker", "tok", None),
        P("worker", "tok", None),
        P("worker", "tok", None),
        P("worker", None),
        P(),
    )
    return jax.shard_map(
        per_device,
        mesh=mesh,
        in_specs=placed,
        out_specs=(P("worker", "tok", None), P("worker", "tok", None)),
        check_vma=False,
    )
```

```python
import functools
import math

import jax
import jax.numpy as jnp
import numpy as np
from jax import lax
from jax.experimental import pallas as pl
from jax.experimental.pallas import tpu as pltpu
from jax.sharding import PartitionSpec as P


D = 2048
KV_WIDTH = 512
ROUNDS = 2
LEARNING_RATE = 0.25
HIGH = lax.Precision.HIGHEST
LANES = 128
CHUNKS = (256, 256, 256, 256)


def flip(value, axis, mask):
    pairs = [(source, source ^ mask) for source in range(lax.axis_size(axis))]
    return lax.ppermute(value, axis, pairs)


def after(value, *others):
    return lax.optimization_barrier((value, *others))[0]


def neighbours(w, workers):
    return (w ^ 1, w ^ 2, (w - 4) % workers, (w + 4) % workers)


def pair_list(workers):
    return [(a, b) for a in range(workers) for b in range(a + 1, workers)]


def update(mine, other, momentum, weights, start):
    cut = slice(start, start + mine.shape[1])
    velocity = 0.5 * momentum[:, cut] + (mine + other)
    return velocity, weights[:, cut] - LEARNING_RATE * velocity


def squares_kernel(workers, block_ref, sums_ref):
    sums_ref[...] = jnp.zeros_like(sums_ref)
    lanes = block_ref.shape[2] // LANES
    for index, (a, b) in enumerate(pair_list(workers)):
        total = None
        for lane in range(lanes):
            cut = slice(lane * LANES, (lane + 1) * LANES)
            gap = block_ref[a, :, cut] - block_ref[b, :, cut]
            part = jnp.sum(gap * gap, axis=0, keepdims=True)
            total = part if total is None else total + part
        sums_ref[index : index + 1, :] = total


def squares(block):
    workers = block.shape[0]
    rows = -(-len(pair_list(workers)) // 8) * 8
    return pl.pallas_call(
        functools.partial(squares_kernel, workers),
        out_shape=jax.ShapeDtypeStruct((rows, LANES), jnp.float32),
        name="squares",
    )(block)


def lane_sums(sums):
    ones = jnp.ones((8, LANES), jnp.float32)
    return lax.dot_general(ones, sums, (((1,), (1,)), ((), ())), precision=HIGH, preferred_element_type=jnp.float32)


def pack_kernel(tokens, owners, me_ref, mix_ref, *rest):
    parts, packed_ref = rest[:-1], rest[-1]
    packed_ref[...] = jnp.zeros_like(packed_ref)
    count = parts[0].shape[0]
    for h in range(2):
        total = None
        for part, owner in zip(parts, owners):
            if owner == h:
                total = part[...] if total is None else total + part[...]
        packed_ref[h : h + 1, 0:count] = lane_sums(total)[0:1]
    lane = lax.broadcasted_iota(jnp.int32, (1, LANES), 1)
    row = jnp.zeros((1, LANES), jnp.float32)
    for k in range(5):
        weight = mix_ref[0, k].astype(jnp.float32) * (1.0 / tokens)
        row = row + jnp.where(lane == me_ref[0] * 5 + k, weight, 0.0)
    packed_ref[2:3, :] = row


def pack(parts, owners, mix_weights, me, tokens):
    smem = pl.BlockSpec(memory_space=pltpu.SMEM)
    vmem = pl.BlockSpec(memory_space=pltpu.VMEM)
    return pl.pallas_call(
        functools.partial(pack_kernel, tokens, owners),
        in_specs=[smem, smem] + [vmem] * len(parts),
        out_specs=vmem,
        out_shape=jax.ShapeDtypeStruct((8, LANES), jnp.float32),
        name="pack",
    )(me.reshape(1), mix_weights, *parts)


def selectors(workers):
    table = np.zeros((5, workers, workers, LANES), np.float32)
    for place, (a, b) in enumerate(pair_list(workers)):
        table[0, a, b, place] = table[0, b, a, place] = 1.0
    for w in range(workers):
        for k, j in enumerate(neighbours(w, workers)):
            table[1, w, j, w * 5 + k + 1] += 1.0
            table[3, j, w, w * 5 + k + 1] += 1.0
        table[2, w, :, w * 5 : w * 5 + 5] = 1.0
        table[4, :, w, w * 5 : w * 5 + 5] = 1.0
    return table.reshape(-1, LANES)


def spread(select, row):
    wide = jnp.broadcast_to(row, (LANES, LANES))
    return lax.dot_general(select, wide, (((1,), (1,)), ((), ())), precision=HIGH, preferred_element_type=jnp.float32)


def mix_kernel(workers, h, starts, clip_ref, packed_ref, select_ref, *rest):
    blocks, out_ref = rest[:-1], rest[-1]
    size = workers * workers
    table = lambda k: select_ref[k * size : (k + 1) * size, :]
    rows_of = lambda flat: [flat[w * workers : (w + 1) * workers] for w in range(workers)]
    mixing = packed_ref[2:3, :]
    share = rows_of(spread(table(1), mixing) / spread(table(2), mixing))
    share_t = rows_of(spread(table(3), mixing) / spread(table(4), mixing))
    place = lax.broadcasted_iota(jnp.int32, (workers, LANES), 0)
    eye = [jnp.where(place == w, 1.0, 0.0) for w in range(workers)]
    radius = [clip_ref[r].astype(jnp.float32) * (math.sqrt(D * KV_WIDTH) / 1000.0) for r in range(ROUNDS)]

    def times(left, right):
        out = []
        for w in range(workers):
            total = None
            for j in range(workers):
                term = left[w][j : j + 1, :] * right[j]
                total = term if total is None else total + term
            out.append(total)
        return out

    first = rows_of(spread(table(0), packed_ref[h : h + 1, :]))
    now, total, total_t = first, None, None
    for r in range(ROUNDS):
        factor = [radius[r] / jnp.maximum(jnp.sqrt(d), radius[r]) for d in now]
        step = [s * f for s, f in zip(share, factor)]
        step = [a + e * (1.0 - jnp.sum(a, axis=0, keepdims=True)) for a, e in zip(step, eye)]
        total = step if total is None else times(step, total)
        if r + 1 < ROUNDS:
            step_t = [s * f for s, f in zip(share_t, factor)]
            keep = 1.0 - functools.reduce(lambda a, b: a + b, step_t)
            step_t = [a + e * keep for a, e in zip(step_t, eye)]
            total_t = step_t if total_t is None else times(total_t, step_t)
            inner = times(times(total, first), total_t)
            diag = functools.reduce(lambda a, b: a + b, [i * e for i, e in zip(inner, eye)])
            now = [
                jnp.maximum(i - 0.5 * (diag + diag[w : w + 1, :]), 0.0) for w, i in enumerate(inner)
            ]
    for block, start in zip(blocks, starts):
        for lane in range(block.shape[2] // LANES):
            cut = slice(lane * LANES, (lane + 1) * LANES)
            into = slice(start + lane * LANES, start + (lane + 1) * LANES)
            old = [block[j, :, cut] for j in range(workers)]
            for w in range(workers):
                value = None
                for j in range(workers):
                    term = total[w][j : j + 1, :] * old[j]
                    value = term if value is None else value + term
                out_ref[w, :, into] = value


def mix(packed, clip_radius, blocks, h, starts, width):
    workers, rows = blocks[0].shape[:2]
    vmem = pl.BlockSpec(memory_space=pltpu.VMEM)
    return pl.pallas_call(
        functools.partial(mix_kernel, workers, h, starts),
        in_specs=[pl.BlockSpec(memory_space=pltpu.SMEM)] + [vmem] * (2 + len(blocks)),
        out_specs=vmem,
        out_shape=jax.ShapeDtypeStruct((workers, rows, width), jnp.float32),
        name="mix",
    )(clip_radius, packed, selectors(workers), *blocks)


def per_device(inputs, cotangent, weights, momentum, mix_weights, clip_radius):
    features, upstream = inputs[0], cotangent[0]
    tokens = lax.axis_size("tok")
    workers = lax.axis_size("worker")
    tok, me = lax.axis_index("tok"), lax.axis_index("worker")
    rows, width = weights.shape[1:]
    half = width // 2
    starts = [sum(CHUNKS[:k]) for k in range(len(CHUNKS))]
    owners = tuple(start // half for start in starts)
    levels = tokens.bit_length() - 1
    count = len(CHUNKS)
    order = [None]

    def partial_rows(offset, k):
        left, right = features, upstream
        if order[0] is not None:
            left, right = lax.optimization_barrier((features, upstream, order[0]))[:2]
        left = lax.dynamic_slice_in_dim(left, (tok ^ offset) * rows, rows, axis=1)
        right = right[:, starts[k] : starts[k] + CHUNKS[k]]
        out = lax.dot_general(left, right, (((0,), (0,)), ((), ())), preferred_element_type=jnp.float32)
        order[0] = out
        return out

    leaves = {}
    last = 1 << (levels - 1)
    for lead in (last, 0):
        for k in range(count + 1):
            for near in (1, 0):
                chunk = k - 1 + near
                if 0 <= chunk < count:
                    for offset in range(lead, lead + last):
                        if offset & 1 == near:
                            leaves[offset, chunk] = partial_rows(offset, chunk)

    def reduced(offset, level, k):
        if level == 0:
            return leaves[offset, k]
        mask = 1 << (level - 1)
        away = reduced(offset ^ mask, level - 1, k)
        away = flip(away, "tok", mask)
        return reduced(offset, level - 1, k) + away

    aways = []
    for k in range(count):
        away = reduced(last, levels - 1, k)
        aways.append(flip(away, "tok", last))
    mines = [reduced(0, levels - 1, k) for k in range(count)]
    mines = [lax.optimization_barrier(mine) for mine in mines]
    velocities, gathered = [], []
    for k in range(count):
        away = after(aways[k], current) if k else after(aways[k], *mines)
        velocity, current = update(mines[k], away, momentum[0], weights[0], starts[k])
        velocities.append(velocity)
        block = current.reshape(workers, rows // workers, CHUNKS[k])
        gathered.append(lax.all_to_all(block, "worker", 0, 0, tiled=True))
    parts = []
    for k in range(count):
        parts.append(squares(gathered[k]))
    packed = pack(parts, owners, mix_weights, me, tokens)
    for axis, size in (("tok", tokens), ("worker", workers)):
        mask = 1
        while mask < size:
            packed = packed + flip(packed, axis, mask)
            mask *= 2
    news = []
    for h in range(2):
        mine = [k for k in range(count) if owners[k] == h]
        blocks, places = [gathered[k] for k in mine], [starts[k] - h * half for k in mine]
        mixed = mix(packed, clip_radius, blocks, h, places, half)
        mixed = lax.all_to_all(mixed, "worker", 0, 0, tiled=True)
        news.append(mixed.reshape(rows, half))
    new, velocity = jnp.concatenate(news, axis=1), jnp.concatenate(velocities, axis=1)
    return new[None], velocity[None]


def solution(mesh):
    placed = (
        P("worker", "tok", None),
        P("worker", "tok", None),
        P("worker", "tok", None),
        P("worker", "tok", None),
        P("worker", None),
        P(),
    )

    return jax.shard_map(
        per_device,
        mesh=mesh,
        in_specs=placed,
        out_specs=(P("worker", "tok", None), P("worker", "tok", None)),
        check_vma=False,
    )
```

```python
import functools
import math

import jax
import jax.numpy as jnp
import numpy as np
from jax import lax
from jax.experimental import pallas as pl
from jax.experimental.pallas import tpu as pltpu
from jax.sharding import PartitionSpec as P


D = 2048
KV_WIDTH = 512
ROUNDS = 2
LEARNING_RATE = 0.25
HIGH = lax.Precision.HIGHEST
LANES = 128
CHUNKS = (256, 256, 256, 256)
STARTS = tuple(sum(CHUNKS[:k]) for k in range(len(CHUNKS)))
COUNT = len(CHUNKS)
EARLY = 2


SMEM = pl.BlockSpec(memory_space=pltpu.SMEM)
VMEM = pl.BlockSpec(memory_space=pltpu.VMEM)


def flip(value, axis, mask):
    pairs = [(source, source ^ mask) for source in range(lax.axis_size(axis))]
    return lax.ppermute(value, axis, pairs)


def after(value, *others):
    return lax.optimization_barrier((value, *others))[0]


def neighbours(w, workers):
    return (w ^ 1, w ^ 2, (w - 4) % workers, (w + 4) % workers)


def pair_list(workers):
    return [(a, b) for a in range(workers) for b in range(a + 1, workers)]


def pair_rows(workers):
    return -(-len(pair_list(workers)) // 8) * 8


def product(left, right):
    return lax.dot_general(left, right, (((0,), (0,)), ((), ())), preferred_element_type=jnp.float32)


def blocks_of(left_ref, upstream_ref, rows, places, outs):
    for i, place in enumerate(places):
        left = left_ref[:, pl.ds(pl.multiple_of(place * rows, LANES), rows)]
        for k in range(COUNT):
            right = upstream_ref[:, STARTS[k] : STARTS[k] + CHUNKS[k]]
            outs[i * COUNT + k][...] = product(left, right)


def first_kernel(rows, cuts, at_ref, features_hbm, upstream_hbm, *rest):
    outs, (left_ref, upstream_ref, sems) = rest[: 2 * COUNT], rest[2 * COUNT :]
    at = at_ref[0]
    columns = pl.ds(pl.multiple_of(at // 2 * (2 * rows), LANES), 2 * rows)
    copies = []
    for i, cut in enumerate(cuts):
        copies.append(pltpu.make_async_copy(features_hbm.at[0, cut, columns], left_ref.at[cut], sems.at[2 * i]))
        copies.append(pltpu.make_async_copy(upstream_hbm.at[0, cut], upstream_ref.at[cut], sems.at[2 * i + 1]))
    for copy in copies:
        copy.start()
    for copy in copies:
        copy.wait()
    side = at % 2
    blocks_of(left_ref, upstream_ref, rows, (1 - side, side), outs)


def second_kernel(rows, at_ref, features_ref, upstream_ref, *outs):
    at = at_ref[0]
    side = at % 2
    blocks_of(features_ref, upstream_ref, rows, (at + 1 - 2 * side, at), outs)


def multiply(at, features, upstream, rows, first):
    outs = [jax.ShapeDtypeStruct((rows, size), jnp.float32) for size in CHUNKS] * 2
    if not first:
        outs = pl.pallas_call(
            functools.partial(second_kernel, rows),
            in_specs=[SMEM, VMEM, VMEM],
            out_specs=[VMEM] * len(outs),
            out_shape=outs,
            compiler_params=pltpu.CompilerParams(vmem_limit_bytes=24 << 20),
            name="second",
        )(at, features[0], upstream[0])
        return list(outs[:COUNT]), list(outs[COUNT:])
    hbm = pl.BlockSpec(memory_space=pltpu.HBM)
    tokens = features.shape[1]
    step = tokens // 6 if tokens % 96 == 0 else tokens
    cuts = [slice(start, start + step) for start in range(0, tokens, step)]
    outs = pl.pallas_call(
        functools.partial(first_kernel, rows, cuts),
        in_specs=[SMEM, hbm, hbm],
        out_specs=[VMEM] * len(outs),
        out_shape=outs,
        scratch_shapes=[
            pltpu.VMEM((tokens, 2 * rows), features.dtype),
            pltpu.VMEM(upstream.shape[1:], upstream.dtype),
            pltpu.SemaphoreType.DMA((2 * len(cuts),)),
        ],
        compiler_params=pltpu.CompilerParams(vmem_limit_bytes=60 << 20),
        name="first",
    )(at, features, upstream)
    return list(outs[:COUNT]), list(outs[COUNT:])


def velocity_kernel(gradient_ref, momentum_ref, *rest):
    rest[-1][...] = 0.5 * momentum_ref[...] + gradient_ref[...]


def velocity_chunk(gradient, momentum, velocity, k):
    rows, width = gradient.shape
    narrow = pl.BlockSpec((rows, width), lambda i: (0, 0))
    wide = pl.BlockSpec((rows, width), lambda i: (0, STARTS[k] // width))
    args, specs, alias = [gradient, momentum], [narrow, wide], {}
    if velocity is not None:
        args.append(velocity)
        specs.append(pl.BlockSpec(memory_space=pl.ANY))
        alias = {2: 0}
    return pl.pallas_call(
        velocity_kernel,
        grid=(1,),
        in_specs=specs,
        out_specs=wide,
        out_shape=jax.ShapeDtypeStruct(momentum.shape, jnp.float32),
        input_output_aliases=alias,
        compiler_params=pltpu.CompilerParams(vmem_limit_bytes=8 << 20),
        name="velocity",
    )(*args)


def update_kernel(k, count, grouped, me_ref, *rest):
    terms, (momentum_ref, weights_ref, gradient_ref, *outs) = rest[:count], rest[count:]
    me = me_ref[0]
    rows = gradient_ref.shape[0]
    cut = slice(STARTS[k], STARTS[k] + CHUNKS[k])
    gradient = terms[0][...]
    for term in terms[1:]:
        gradient = gradient + term[...]
    gradient_ref[...] = gradient
    current = weights_ref[:, cut] - LEARNING_RATE * (0.5 * momentum_ref[:, cut] + gradient)
    size = outs[0].shape[0]
    parts = rows // size
    for place in range(parts):
        if grouped:
            for mask, out in enumerate(outs):

                @pl.when((me >= grouped) == ((place ^ mask) == 1))
                def _(out=out, place=place):
                    out[...] = current[place * size : (place + 1) * size]

        else:
            for mask, out in enumerate(outs):

                @pl.when((me ^ mask) == place)
                def _(out=out, place=place):
                    out[...] = current[place * size : (place + 1) * size]


def update(me, terms, momentum, weights, k, group, grouped):
    rows = terms[0].shape[0]
    parts = 2 if grouped else 2 * group
    full = jax.ShapeDtypeStruct(terms[0].shape, jnp.float32)
    cut = jax.ShapeDtypeStruct((rows // parts, CHUNKS[k]), jnp.float32)
    gradient, *outs = pl.pallas_call(
        functools.partial(update_kernel, k, len(terms), group if grouped else 0),
        in_specs=[SMEM] + [VMEM] * (len(terms) + 2),
        out_specs=[VMEM] * (1 + parts),
        out_shape=[full] + [cut] * parts,
        compiler_params=pltpu.CompilerParams(vmem_limit_bytes=8 << 20),
        name="update",
    )(me, *terms, momentum, weights)
    return gradient, outs


def regroup_kernel(group, me_ref, keep_ref, got_ref, *outs):
    rank = me_ref[0] % group
    size = outs[0].shape[1]
    for mask, out in enumerate(outs):
        cut = pl.ds(pl.multiple_of((rank ^ mask) * size, 8), size)
        out[0] = keep_ref[cut, :]
        out[1] = got_ref[cut, :]


def regroup(me, keep, got, group):
    rows, width = keep.shape
    return pl.pallas_call(
        functools.partial(regroup_kernel, group),
        in_specs=[SMEM, VMEM, VMEM],
        out_specs=[VMEM] * group,
        out_shape=[jax.ShapeDtypeStruct((2, rows // group, width), jnp.float32)] * group,
        compiler_params=pltpu.CompilerParams(vmem_limit_bytes=8 << 20),
        name="regroup",
    )(me, keep, got)


def pieces_of(refs, cut):
    if len(refs[0].shape) == 2:
        return [ref[:, cut] for ref in refs]
    return [ref[half, :, cut] for half in range(2) for ref in refs]


def gap_row(left, right):
    gap = left - right
    return jnp.sum(gap * gap, axis=0, keepdims=True)


def add_squares(refs, h_of, rows, sums_ref):
    for lane, h in enumerate(h_of):
        old = pieces_of(refs, slice(lane * LANES, (lane + 1) * LANES))
        for place, (a, b) in enumerate(pair_list(len(old))):
            at = slice(h * rows + place, h * rows + place + 1)
            sums_ref[at, :] = sums_ref[at, :] + gap_row(old[a], old[b])


def squares_kernel(h_of, *rest):
    refs, sums_ref = rest[:-1], rest[-1]
    sums_ref[...] = jnp.zeros_like(sums_ref)
    add_squares(refs, h_of, sums_ref.shape[0] // 2, sums_ref)


def squares(pieces, workers, h_of):
    return pl.pallas_call(
        functools.partial(squares_kernel, h_of),
        in_specs=[VMEM] * len(pieces),
        out_specs=VMEM,
        out_shape=jax.ShapeDtypeStruct((2 * pair_rows(workers), LANES), jnp.float32),
        compiler_params=pltpu.CompilerParams(vmem_limit_bytes=4 << 20),
        name="squares",
    )(*pieces)


def lane_sums(sums):
    ones = jnp.ones((8, LANES), jnp.float32)
    return lax.dot_general(ones, sums, (((1,), (1,)), ((), ())), precision=HIGH, preferred_element_type=jnp.float32)


def pack_kernel(workers, tokens, parts, h_of, me_ref, mix_ref, *rest):
    rows = pair_rows(workers)
    sums, refs = rest[:parts], rest[parts:-3]
    packed_ref, table_ref, total_ref = rest[-3:]
    me = me_ref[0]
    total = sums[0][...]
    for part in sums[1:]:
        total = total + part[...]
    total_ref[...] = total
    add_squares(refs, h_of, rows, total_ref)
    packed_ref[...] = jnp.zeros_like(packed_ref)
    for h in range(2):
        for place, (a, b) in enumerate(pair_list(workers)):
            row = total_ref[h * rows + place : h * rows + place + 1, :]
            table_ref[a * workers + b : a * workers + b + 1, :] = row
            table_ref[b * workers + a : b * workers + a + 1, :] = row
        for place, (a, b) in enumerate(pair_list(workers)):
            row = table_ref[pl.ds((a ^ me) * workers + (b ^ me), 1), :]
            total_ref[h * rows + place : h * rows + place + 1, :] = row
        packed_ref[h : h + 1, 0:rows] = lane_sums(total_ref[h * rows : (h + 1) * rows, :])[0:1]
    lane = lax.broadcasted_iota(jnp.int32, (1, LANES), 1)
    row = jnp.zeros((1, LANES), jnp.float32)
    for k in range(5):
        weight = mix_ref[0, k].astype(jnp.float32) * (1.0 / tokens)
        row = row + jnp.where(lane == me * 5 + k, weight, 0.0)
    packed_ref[2:3, :] = row


def pack(sums, pieces, mix_weights, me, workers, tokens, h_of):
    return pl.pallas_call(
        functools.partial(pack_kernel, workers, tokens, len(sums), h_of),
        in_specs=[SMEM, SMEM] + [VMEM] * (len(sums) + len(pieces)),
        out_specs=VMEM,
        out_shape=jax.ShapeDtypeStruct((8, LANES), jnp.float32),
        scratch_shapes=[
            pltpu.VMEM((workers * workers, LANES), jnp.float32),
            pltpu.VMEM((2 * pair_rows(workers), LANES), jnp.float32),
        ],
        compiler_params=pltpu.CompilerParams(vmem_limit_bytes=4 << 20),
        name="pack",
    )(me, mix_weights, *sums, *pieces)


def selectors(workers):
    table = np.zeros((5, workers, workers, LANES), np.float32)
    for place, (a, b) in enumerate(pair_list(workers)):
        table[0, a, b, place] = table[0, b, a, place] = 1.0
    for w in range(workers):
        for k, j in enumerate(neighbours(w, workers)):
            table[1, w, j, w * 5 + k + 1] += 1.0
            table[3, j, w, w * 5 + k + 1] += 1.0
        table[2, w, :, w * 5 : w * 5 + 5] = 1.0
        table[4, :, w, w * 5 : w * 5 + 5] = 1.0
    return table.reshape(-1, LANES)


def spread(select, row):
    wide = jnp.broadcast_to(row, (LANES, LANES))
    return lax.dot_general(select, wide, (((1,), (1,)), ((), ())), precision=HIGH, preferred_element_type=jnp.float32)


def fill_matrices(workers, clip_ref, packed_ref, select_ref, matrix_ref):
    size = workers * workers
    table = lambda k: select_ref[k * size : (k + 1) * size, :]
    rows_of = lambda flat: [flat[w * workers : (w + 1) * workers] for w in range(workers)]
    mixing = packed_ref[2:3, :]
    share = rows_of(spread(table(1), mixing) / spread(table(2), mixing))
    share_t = rows_of(spread(table(3), mixing) / spread(table(4), mixing))
    place = lax.broadcasted_iota(jnp.int32, (workers, LANES), 0)
    eye = [jnp.where(place == w, 1.0, 0.0) for w in range(workers)]
    radius = [clip_ref[r].astype(jnp.float32) * (math.sqrt(D * KV_WIDTH) / 1000.0) for r in range(ROUNDS)]

    def times(left, right):
        out = []
        for w in range(workers):
            total = None
            for j in range(workers):
                term = left[w][j : j + 1, :] * right[j]
                total = term if total is None else total + term
            out.append(total)
        return out

    for h in range(2):
        first = rows_of(spread(table(0), packed_ref[h : h + 1, :]))
        now, total, total_t = first, None, None
        for r in range(ROUNDS):
            factor = [radius[r] / jnp.maximum(jnp.sqrt(d), radius[r]) for d in now]
            step = [s * f for s, f in zip(share, factor)]
            step = [a + e * (1.0 - jnp.sum(a, axis=0, keepdims=True)) for a, e in zip(step, eye)]
            total = step if total is None else times(step, total)
            if r + 1 < ROUNDS:
                step_t = [s * f for s, f in zip(share_t, factor)]
                keep = 1.0 - functools.reduce(lambda a, b: a + b, step_t)
                step_t = [a + e * keep for a, e in zip(step_t, eye)]
                total_t = step_t if total_t is None else times(total_t, step_t)
                inner = times(times(total, first), total_t)
                diag = functools.reduce(lambda a, b: a + b, [i * e for i, e in zip(inner, eye)])
                now = [
                    jnp.maximum(i - 0.5 * (diag + diag[w : w + 1, :]), 0.0) for w, i in enumerate(inner)
                ]
        for w in range(workers):
            at = h * size + w * workers
            matrix_ref[at : at + workers, :] = total[w]


def mix_kernel(workers, half, counts, masks, first, me_ref, *rest):
    if first:
        clip_ref, packed_ref, select_ref, *rest = rest
        matrix_ref, *rest = rest[-1:] + rest[:-1]
        fill_matrices(workers, clip_ref, packed_ref, select_ref, matrix_ref)
    else:
        matrix_ref, *rest = rest
    chunks = []
    for count in counts:
        chunks.append(rest[:count])
        rest = rest[count:]
    me = me_ref[0]
    for k, refs in enumerate(chunks):
        for lane in range(CHUNKS[k] // LANES):
            start = STARTS[k] + lane * LANES
            base = start // half * workers * workers
            old = pieces_of(refs, slice(lane * LANES, (lane + 1) * LANES))
            for mask, out in zip(masks, rest):
                value = None
                for other, rows in enumerate(old):
                    share = matrix_ref[pl.ds(base + (me ^ mask) * workers + (me ^ other), 1), :]
                    value = share * rows if value is None else value + share * rows
                out[:, start : start + LANES] = value


def mix(masks, me, matrix, clip_radius, packed, chunks, workers, rows, width):
    first = matrix is None
    table = jax.ShapeDtypeStruct((2 * workers * workers, LANES), jnp.float32)
    piece = jax.ShapeDtypeStruct((rows, width), jnp.float32)
    head = (clip_radius, packed, selectors(workers)) if first else (matrix,)
    counts = [len(chunk) for chunk in chunks]
    return pl.pallas_call(
        functools.partial(mix_kernel, workers, width // 2, counts, masks, first),
        in_specs=[SMEM] + ([SMEM] if first else []) + [VMEM] * (len(head) - first + sum(counts)),
        out_specs=[VMEM] * (len(masks) + first),
        out_shape=[piece] * len(masks) + [table] * first,
        compiler_params=pltpu.CompilerParams(vmem_limit_bytes=16 << 20),
        name="mix",
    )(me, *head, *[piece for chunk in chunks for piece in chunk])


def per_device(inputs, cotangent, weights, momentum, mix_weights, clip_radius):
    tokens = lax.axis_size("tok")
    workers = lax.axis_size("worker")
    group = workers // 2
    tok, me = lax.axis_index("tok"), lax.axis_index("worker")
    here = me.reshape(1)
    rows, width = weights.shape[1:]
    piece = rows // workers
    half = width // 2
    h_of = [tuple((start + lane) // half for lane in range(0, size, LANES)) for start, size in zip(STARTS, CHUNKS)]
    levels = tokens.bit_length() - 1
    order = [None]

    last = 1 << (levels - 1)
    index = lambda offset: (tok ^ offset).reshape(1)
    leaves = {}
    for offset in [*range(last, tokens, 2), *range(0, last, 2)]:
        at = index(offset) if order[0] is None else after(index(offset), order[0])
        leaves[offset + 1], leaves[offset] = multiply(at, inputs, cotangent, rows, order[0] is None)
        order[0] = leaves[offset][0]

    def arrived(offset, level, k):
        terms = []
        for step in range(1, level + 1):
            mask = 1 << (step - 1)
            away = reduced(offset ^ mask, step - 1, k)
            terms.append(flip(away, "tok", mask))
        return terms

    def reduced(offset, level, k):
        return sum(arrived(offset, level, k), leaves[offset][k])

    def send_terms(k, *gates):
        leaves[last][k] = after(leaves[last][k], *gates)
        away = reduced(last, levels - 1, k)
        return flip(away, "tok", last), away

    aways, away = [], leaves[last][0]
    for k in range(EARLY):
        moved, away = send_terms(k, away)
        aways.append(moved)
    extras = [arrived(0, levels - 1, k) for k in range(COUNT)]
    velocity, chunks, sums = None, [], []
    for k in range(COUNT):
        grouped = k < COUNT - 1
        away = after(aways[k], gradient) if k else aways[k]
        terms = [leaves[0][k], *extras[k], away]
        gradient, outs = update(here, terms, momentum[0], weights[0], k, group, grouped)
        if grouped:
            got = flip(outs[1], "worker", group)
            pieces = list(regroup(here, outs[0], got, group))
            for mask in range(1, group):
                pieces[mask] = flip(pieces[mask], "worker", mask)
            sums.append(squares(pieces, workers, h_of[k]))
        else:
            pieces = list(outs)
            for mask in [*range(group, workers), *range(1, group)]:
                pieces[mask] = flip(pieces[mask], "worker", mask)
        chunks.append(pieces)
        if len(aways) < COUNT:
            moved, _ = send_terms(len(aways), gradient)
            aways.append(moved)
        velocity = velocity_chunk(gradient, momentum[0], velocity, k)
    packed = pack(sums, chunks[-1], mix_weights, here, workers, tokens, h_of[-1])
    for axis, size in (("tok", tokens), ("worker", workers)):
        mask = 1
        while mask < size:
            packed = packed + flip(packed, axis, mask)
            mask *= 2
    news = {}
    far = tuple(range(group, workers))
    *pieces, matrix = mix(far, here, None, clip_radius, packed, chunks, workers, piece, width)
    for mask, value in zip(far, pieces):
        news[mask] = flip(value, "worker", mask)
    near = tuple(range(group))
    pieces = mix(near, here, matrix, clip_radius, packed, chunks, workers, piece, width)
    news[0] = pieces[0]
    for mask in near[1:]:
        news[mask] = flip(pieces[mask], "worker", mask)
    new = jnp.zeros((rows, width), jnp.float32)
    for mask in [*near, *far]:
        new = lax.dynamic_update_slice_in_dim(new, news[mask], (me ^ mask) * piece, 0)
    return new[None], velocity[None]


def solution(mesh):
    placed = (
        P("worker", "tok", None),
        P("worker", "tok", None),
        P("worker", "tok", None),
        P("worker", "tok", None),
        P("worker", None),
        P(),
    )

    return jax.shard_map(
        per_device,
        mesh=mesh,
        in_specs=placed,
        out_specs=(P("worker", "tok", None), P("worker", "tok", None)),
        check_vma=False,
    )
```

```python
import functools
import math

import jax
import jax.numpy as jnp
import numpy as np
from jax import lax
from jax.experimental import pallas as pl
from jax.experimental.pallas import tpu as pltpu
from jax.sharding import PartitionSpec as P


D = 2048
KV_WIDTH = 512
ROUNDS = 2
LEARNING_RATE = 0.25
HIGH = lax.Precision.HIGHEST
LANES = 128
CHUNKS = (256, 256, 256, 256)
STARTS = tuple(sum(CHUNKS[:k]) for k in range(len(CHUNKS)))
COUNT = len(CHUNKS)
EARLY = 2
BITS = (-1, 0, 0, 0)
SHARED = 3


SMEM = pl.BlockSpec(memory_space=pltpu.SMEM)
VMEM = pl.BlockSpec(memory_space=pltpu.VMEM)


def flip(value, axis, mask):
    pairs = [(source, source ^ mask) for source in range(lax.axis_size(axis))]
    return lax.ppermute(value, axis, pairs)


def after(value, *others):
    return lax.optimization_barrier((value, *others))[0]


def neighbours(w, workers):
    return (w ^ 1, w ^ 2, (w - 4) % workers, (w + 4) % workers)


def pair_list(workers):
    return [(a, b) for a in range(workers) for b in range(a + 1, workers)]


def pair_rows(workers):
    return -(-len(pair_list(workers)) // 8) * 8


def product(left, right):
    return lax.dot_general(left, right, (((0,), (0,)), ((), ())), preferred_element_type=jnp.float32)


def blocks_of(left_ref, upstream_ref, rows, places, outs):
    for i, place in enumerate(places):
        left = left_ref[:, pl.ds(pl.multiple_of(place * rows, LANES), rows)]
        for k in range(COUNT):
            right = upstream_ref[:, STARTS[k] : STARTS[k] + CHUNKS[k]]
            outs[i * COUNT + k][...] = product(left, right)


def first_kernel(rows, cuts, at_ref, features_hbm, upstream_hbm, *rest):
    outs, (left_ref, upstream_ref, sems) = rest[: 2 * COUNT], rest[2 * COUNT :]
    at = at_ref[0]
    columns = pl.ds(pl.multiple_of(at // 2 * (2 * rows), LANES), 2 * rows)
    copies = []
    for i, cut in enumerate(cuts):
        copies.append(pltpu.make_async_copy(features_hbm.at[0, cut, columns], left_ref.at[cut], sems.at[2 * i]))
        copies.append(pltpu.make_async_copy(upstream_hbm.at[0, cut], upstream_ref.at[cut], sems.at[2 * i + 1]))
    for copy in copies:
        copy.start()
    for copy in copies:
        copy.wait()
    side = at % 2
    blocks_of(left_ref, upstream_ref, rows, (1 - side, side), outs)


def second_kernel(rows, at_ref, features_ref, upstream_ref, *outs):
    at = at_ref[0]
    side = at % 2
    blocks_of(features_ref, upstream_ref, rows, (at + 1 - 2 * side, at), outs)


def multiply(at, features, upstream, rows, first):
    outs = [jax.ShapeDtypeStruct((rows, size), jnp.float32) for size in CHUNKS] * 2
    if not first:
        outs = pl.pallas_call(
            functools.partial(second_kernel, rows),
            in_specs=[SMEM, VMEM, VMEM],
            out_specs=[VMEM] * len(outs),
            out_shape=outs,
            compiler_params=pltpu.CompilerParams(vmem_limit_bytes=54 << 20),
            name="second",
        )(at, features[0], upstream[0])
        return list(outs[:COUNT]), list(outs[COUNT:])
    hbm = pl.BlockSpec(memory_space=pltpu.HBM)
    tokens = features.shape[1]
    step = tokens // 6 if tokens % 96 == 0 else tokens
    cuts = [slice(start, start + step) for start in range(0, tokens, step)]
    outs = pl.pallas_call(
        functools.partial(first_kernel, rows, cuts),
        in_specs=[SMEM, hbm, hbm],
        out_specs=[VMEM] * len(outs),
        out_shape=outs,
        scratch_shapes=[
            pltpu.VMEM((tokens, 2 * rows), features.dtype),
            pltpu.VMEM(upstream.shape[1:], upstream.dtype),
            pltpu.SemaphoreType.DMA((2 * len(cuts),)),
        ],
        compiler_params=pltpu.CompilerParams(vmem_limit_bytes=59 << 20),
        name="first",
    )(at, features, upstream)
    return list(outs[:COUNT]), list(outs[COUNT:])


def velocity_kernel(cut, gradient_ref, momentum_ref, *rest):
    out_ref, scratch_ref, sem = rest[-3:]
    scratch_ref[...] = 0.5 * momentum_ref[:, cut] + gradient_ref[...]
    copy = pltpu.make_async_copy(scratch_ref, out_ref.at[:, cut], sem)
    copy.start()
    copy.wait()


def velocity_chunk(gradient, momentum, velocity, k):
    hbm = pl.BlockSpec(memory_space=pl.ANY)
    cut = slice(STARTS[k], STARTS[k] + CHUNKS[k])
    more = () if velocity is None else (velocity,)
    return pl.pallas_call(
        functools.partial(velocity_kernel, cut),
        in_specs=[VMEM, VMEM] + [hbm] * len(more),
        out_specs=hbm,
        out_shape=jax.ShapeDtypeStruct(momentum.shape, jnp.float32),
        scratch_shapes=[pltpu.VMEM(gradient.shape, jnp.float32), pltpu.SemaphoreType.DMA],
        input_output_aliases={2: 0} if more else {},
        compiler_params=pltpu.CompilerParams(vmem_limit_bytes=8 << 20),
        name="velocity",
    )(gradient, momentum, *more)


def without(value, bit):
    return (value >> (bit + 1)) << bit | value & ((1 << bit) - 1)


def spread_bits(value, bit):
    return (value >> bit) << (bit + 1) | value & ((1 << bit) - 1)


def update_kernel(k, count, bit, me_ref, *rest):
    terms, (momentum_ref, weights_ref, gradient_ref, keep_ref, send_ref) = rest[:count], rest[count:]
    cut = slice(STARTS[k], STARTS[k] + CHUNKS[k])
    gradient = terms[0][...]
    for term in terms[1:]:
        gradient = gradient + term[...]
    gradient_ref[...] = gradient
    current = weights_ref[:, cut] - LEARNING_RATE * (0.5 * momentum_ref[:, cut] + gradient)
    side = (me_ref[0] >> bit) & 1
    slots, size, _ = keep_ref.shape
    for worker in range(2 * slots):
        piece = current[worker * size : (worker + 1) * size]
        for out, mine in ((keep_ref, worker >> bit & 1), (send_ref, 1 - (worker >> bit & 1))):

            @pl.when(side == mine)
            def _(out=out, piece=piece, slot=without(worker, bit)):
                out[slot] = piece


def update(me, terms, momentum, weights, k, workers, bit):
    rows = terms[0].shape[0]
    full = jax.ShapeDtypeStruct(terms[0].shape, jnp.float32)
    part = jax.ShapeDtypeStruct((workers // 2, rows // workers, CHUNKS[k]), jnp.float32)
    return pl.pallas_call(
        functools.partial(update_kernel, k, len(terms), bit),
        in_specs=[SMEM] + [VMEM] * (len(terms) + 2),
        out_specs=[VMEM] * 3,
        out_shape=[full, part, part],
        compiler_params=pltpu.CompilerParams(vmem_limit_bytes=8 << 20),
        name="update",
    )(me, *terms, momentum, weights)


def regroup_kernel(bit, turn, me_ref, *rest):
    group = rest[0].shape[0]
    parts, outs = rest[:-group], rest[-group:]
    rank = without(me_ref[0], bit) ^ turn
    for i, out in enumerate(outs):
        start = 0
        for place in range(0, len(parts), 2):
            width = parts[place].shape[2]
            for side in range(2):
                out[side, :, start : start + width] = parts[place + side][rank ^ i]
            start += width


def regroup(me, parts, bit, turn=0):
    group, rows, _ = parts[0].shape
    width = sum(part.shape[2] for part in parts[::2])
    return pl.pallas_call(
        functools.partial(regroup_kernel, bit, turn),
        in_specs=[SMEM] + [VMEM] * len(parts),
        out_specs=[VMEM] * group,
        out_shape=[jax.ShapeDtypeStruct((2, rows, width), jnp.float32)] * group,
        compiler_params=pltpu.CompilerParams(vmem_limit_bytes=8 << 20),
        name="regroup",
    )(me, *parts)


def pieces_of(refs, bit, cut):
    masks = range(2 * len(refs))
    return [refs[without(mask, bit)][mask >> bit & 1, :, cut] for mask in masks]


def gap_row(left, right):
    gap = left - right
    return jnp.sum(gap * gap, axis=0, keepdims=True)


def add_squares(refs, bit, h_of, rows, sums_ref):
    for lane, h in enumerate(h_of):
        old = pieces_of(refs, bit, slice(lane * LANES, (lane + 1) * LANES))
        for place, (a, b) in enumerate(pair_list(len(old))):
            at = slice(h * rows + place, h * rows + place + 1)
            sums_ref[at, :] = sums_ref[at, :] + gap_row(old[a], old[b])


def squares_kernel(bit, h_of, *rest):
    refs, sums_ref = rest[:-1], rest[-1]
    sums_ref[...] = jnp.zeros_like(sums_ref)
    add_squares(refs, bit, h_of, sums_ref.shape[0] // 2, sums_ref)


def squares(pieces, workers, bit, h_of):
    return pl.pallas_call(
        functools.partial(squares_kernel, bit, h_of),
        in_specs=[VMEM] * len(pieces),
        out_specs=VMEM,
        out_shape=jax.ShapeDtypeStruct((2 * pair_rows(workers), LANES), jnp.float32),
        compiler_params=pltpu.CompilerParams(vmem_limit_bytes=4 << 20),
        name="squares",
    )(*pieces)


def lane_sums(sums):
    ones = jnp.ones((8, LANES), jnp.float32)
    return lax.dot_general(ones, sums, (((1,), (1,)), ((), ())), precision=HIGH, preferred_element_type=jnp.float32)


def pack_kernel(workers, tokens, parts, bit, h_of, me_ref, mix_ref, *rest):
    rows = pair_rows(workers)
    sums, refs = rest[:parts], rest[parts:-3]
    packed_ref, table_ref, total_ref = rest[-3:]
    me = me_ref[0]
    total = sums[0][...]
    for part in sums[1:]:
        total = total + part[...]
    total_ref[...] = total
    add_squares(refs, bit, h_of, rows, total_ref)
    packed_ref[...] = jnp.zeros_like(packed_ref)
    for h in range(2):
        for place, (a, b) in enumerate(pair_list(workers)):
            row = total_ref[h * rows + place : h * rows + place + 1, :]
            table_ref[a * workers + b : a * workers + b + 1, :] = row
            table_ref[b * workers + a : b * workers + a + 1, :] = row
        for place, (a, b) in enumerate(pair_list(workers)):
            row = table_ref[pl.ds((a ^ me) * workers + (b ^ me), 1), :]
            total_ref[h * rows + place : h * rows + place + 1, :] = row
        packed_ref[h : h + 1, 0:rows] = lane_sums(total_ref[h * rows : (h + 1) * rows, :])[0:1]
    lane = lax.broadcasted_iota(jnp.int32, (1, LANES), 1)
    row = jnp.zeros((1, LANES), jnp.float32)
    for k in range(5):
        weight = mix_ref[0, k].astype(jnp.float32) * (1.0 / tokens)
        row = row + jnp.where(lane == me * 5 + k, weight, 0.0)
    packed_ref[2:3, :] = row


def pack(sums, pieces, mix_weights, me, workers, tokens, bit, h_of):
    return pl.pallas_call(
        functools.partial(pack_kernel, workers, tokens, len(sums), bit, h_of),
        in_specs=[SMEM, SMEM] + [VMEM] * (len(sums) + len(pieces)),
        out_specs=VMEM,
        out_shape=jax.ShapeDtypeStruct((8, LANES), jnp.float32),
        scratch_shapes=[
            pltpu.VMEM((workers * workers, LANES), jnp.float32),
            pltpu.VMEM((2 * pair_rows(workers), LANES), jnp.float32),
        ],
        compiler_params=pltpu.CompilerParams(vmem_limit_bytes=4 << 20),
        name="pack",
    )(me, mix_weights, *sums, *pieces)


def selectors(workers):
    table = np.zeros((5, workers, workers, LANES), np.float32)
    for place, (a, b) in enumerate(pair_list(workers)):
        table[0, a, b, place] = table[0, b, a, place] = 1.0
    for w in range(workers):
        for k, j in enumerate(neighbours(w, workers)):
            table[1, w, j, w * 5 + k + 1] += 1.0
            table[3, j, w, w * 5 + k + 1] += 1.0
        table[2, w, :, w * 5 : w * 5 + 5] = 1.0
        table[4, :, w, w * 5 : w * 5 + 5] = 1.0
    return table.reshape(-1, LANES)


def spread(select, row):
    wide = jnp.broadcast_to(row, (LANES, LANES))
    return lax.dot_general(select, wide, (((1,), (1,)), ((), ())), precision=HIGH, preferred_element_type=jnp.float32)


def fill_matrices(workers, clip_ref, packed_ref, select_ref, matrix_ref):
    size = workers * workers
    table = lambda k: select_ref[k * size : (k + 1) * size, :]
    rows_of = lambda flat: [flat[w * workers : (w + 1) * workers] for w in range(workers)]
    mixing = packed_ref[2:3, :]
    share = rows_of(spread(table(1), mixing) / spread(table(2), mixing))
    share_t = rows_of(spread(table(3), mixing) / spread(table(4), mixing))
    place = lax.broadcasted_iota(jnp.int32, (workers, LANES), 0)
    eye = [jnp.where(place == w, 1.0, 0.0) for w in range(workers)]
    radius = [clip_ref[r].astype(jnp.float32) * (math.sqrt(D * KV_WIDTH) / 1000.0) for r in range(ROUNDS)]

    def times(left, right):
        out = []
        for w in range(workers):
            total = None
            for j in range(workers):
                term = left[w][j : j + 1, :] * right[j]
                total = term if total is None else total + term
            out.append(total)
        return out

    for h in range(2):
        first = rows_of(spread(table(0), packed_ref[h : h + 1, :]))
        now, total, total_t = first, None, None
        for r in range(ROUNDS):
            factor = [radius[r] / jnp.maximum(jnp.sqrt(d), radius[r]) for d in now]
            step = [s * f for s, f in zip(share, factor)]
            step = [a + e * (1.0 - jnp.sum(a, axis=0, keepdims=True)) for a, e in zip(step, eye)]
            total = step if total is None else times(step, total)
            if r + 1 < ROUNDS:
                step_t = [s * f for s, f in zip(share_t, factor)]
                keep = 1.0 - functools.reduce(lambda a, b: a + b, step_t)
                step_t = [a + e * keep for a, e in zip(step_t, eye)]
                total_t = step_t if total_t is None else times(total_t, step_t)
                inner = times(times(total, first), total_t)
                diag = functools.reduce(lambda a, b: a + b, [i * e for i, e in zip(inner, eye)])
                now = [
                    jnp.maximum(i - 0.5 * (diag + diag[w : w + 1, :]), 0.0) for w, i in enumerate(inner)
                ]
        for w in range(workers):
            at = h * size + w * workers
            matrix_ref[at : at + workers, :] = total[w]


def mix_kernel(workers, half, layout, masks, first, me_ref, *rest):
    if first:
        clip_ref, packed_ref, select_ref, *rest = rest
        matrix_ref, *rest = rest[-1:] + rest[:-1]
        fill_matrices(workers, clip_ref, packed_ref, select_ref, matrix_ref)
    else:
        matrix_ref, *rest = rest
    me = me_ref[0]
    for bit, start, into in layout:
        refs, rest = rest[: workers // 2], rest[workers // 2 :]
        for lane in range(0, refs[0].shape[2], LANES):
            base = (start + lane) // half * workers * workers
            old = pieces_of(refs, bit, slice(lane, lane + LANES))
            for mask, out in zip(masks, rest[-len(masks) :]):
                value = None
                for other, rows in enumerate(old):
                    share = matrix_ref[pl.ds(base + (me ^ mask) * workers + (me ^ other), 1), :]
                    value = share * rows if value is None else value + share * rows
                out[:, into + lane : into + lane + LANES] = value


def mix(masks, me, matrix, head, chunks, layout, workers, half):
    first = matrix is None
    rows = chunks[0][0].shape[1]
    width = sum(chunk[0].shape[2] for chunk in chunks)
    table = jax.ShapeDtypeStruct((2 * workers * workers, LANES), jnp.float32)
    head = (*head, selectors(workers)) if first else (matrix,)
    return pl.pallas_call(
        functools.partial(mix_kernel, workers, half, layout, masks, first),
        in_specs=[SMEM] * (1 + first) + [VMEM] * (len(head) - first + sum(len(chunk) for chunk in chunks)),
        out_specs=[VMEM] * (len(masks) + first),
        out_shape=[jax.ShapeDtypeStruct((rows, width), jnp.float32)] * len(masks) + [table] * first,
        compiler_params=pltpu.CompilerParams(vmem_limit_bytes=16 << 20),
        name="mix",
    )(me, *head, *[piece for chunk in chunks for piece in chunk])


def place_kernel(spots, me_ref, *rest):
    pieces, out_ref, sems = rest[:-2], rest[-2], rest[-1]
    copies = []
    for i, (mask, start) in enumerate(spots):
        rows, width = pieces[i].shape
        at = pl.ds(pl.multiple_of((me_ref[0] ^ mask) * rows, 8), rows)
        copies.append(pltpu.make_async_copy(pieces[i], out_ref.at[at, start : start + width], sems.at[i]))
        copies[i].start()
    for copy in copies:
        copy.wait()


def place(me, pieces, spots, rows, width):
    return pl.pallas_call(
        functools.partial(place_kernel, spots),
        in_specs=[SMEM] + [pl.BlockSpec(memory_space=pl.ANY)] * len(pieces),
        out_specs=pl.BlockSpec(memory_space=pl.ANY),
        out_shape=jax.ShapeDtypeStruct((rows, width), jnp.float32),
        scratch_shapes=[pltpu.SemaphoreType.DMA((len(pieces),))],
        compiler_params=pltpu.CompilerParams(vmem_limit_bytes=4 << 20),
        name="place",
    )(me, *pieces)


def per_device(inputs, cotangent, weights, momentum, mix_weights, clip_radius):
    tokens = lax.axis_size("tok")
    workers = lax.axis_size("worker")
    group = workers // 2
    tok, me = lax.axis_index("tok"), lax.axis_index("worker")
    here = me.reshape(1)
    rows, width = weights.shape[1:]
    half = width // 2
    h_of = [tuple((start + lane) // half for lane in range(0, size, LANES)) for start, size in zip(STARTS, CHUNKS)]
    levels = tokens.bit_length() - 1
    order = [None]

    last = 1 << (levels - 1)
    index = lambda offset: (tok ^ offset).reshape(1)
    leaves = {}
    for offset in [*range(last, tokens, 2), *range(0, last, 2)]:
        at = index(offset) if order[0] is None else after(index(offset), order[0])
        leaves[offset + 1], leaves[offset] = multiply(at, inputs, cotangent, rows, order[0] is None)
        order[0] = leaves[offset][0]

    def arrived(offset, level, k):
        terms = []
        for step in range(1, level + 1):
            mask = 1 << (step - 1)
            away = reduced(offset ^ mask, step - 1, k)
            terms.append(flip(away, "tok", mask))
        return terms

    def reduced(offset, level, k):
        return sum(arrived(offset, level, k), leaves[offset][k])

    def send_terms(k, *gates):
        leaves[last][k] = after(leaves[last][k], *gates)
        away = reduced(last, levels - 1, k)
        return flip(away, "tok", last), away

    aways, away = [], leaves[last][0]
    for k in range(EARLY):
        moved, away = send_terms(k, away)
        aways.append(moved)
    extras = [arrived(0, levels - 1, k) for k in range(COUNT)]
    velocity, chunks, sums = None, [], []
    bits = [bit % (workers.bit_length() - 1) for bit in BITS]
    held = []
    for k in range(COUNT):
        away = after(aways[k], gradient) if k else aways[k]
        terms = [leaves[0][k], *extras[k], away]
        gradient, keep, send = update(here, terms, momentum[0], weights[0], k, workers, bits[k])
        got = flip(send, "worker", 1 << bits[k])
        pieces = list(regroup(here, (keep, got), bits[k]))
        if k >= SHARED:
            held += [keep, got]
        for i in reversed(range(1, group)):
            pieces[i] = flip(pieces[i], "worker", spread_bits(i, bits[k]))
        chunks.append(pieces)
        if k < COUNT - 1:
            sums.append(squares(pieces, workers, bits[k], h_of[k]))
        if k == 0:
            moved, _ = send_terms(len(aways), gradient)
            aways.append(moved)
        velocity = velocity_chunk(gradient, momentum[0], velocity, k)
        if 0 < k and len(aways) < COUNT:
            moved, _ = send_terms(len(aways), velocity)
            aways.append(moved)
    packed = pack(sums, chunks[-1], mix_weights, here, workers, tokens, bits[-1], h_of[-1])
    bit = bits[SHARED]
    mirror = list(regroup(here, held, bit, without(group, bit)))
    later = [*range(group // 2, group), *range(1, group // 2)]
    for axis, size in (("tok", tokens), ("worker", workers)):
        mask = 1
        while mask < size:
            packed = packed + flip(packed, axis, mask)
            if later:
                i = later.pop(0)
                mirror[i] = flip(after(mirror[i], packed), "worker", spread_bits(i, bit))
            mask *= 2
    for i in later:
        mirror[i] = flip(mirror[i], "worker", spread_bits(i, bit))
    split = STARTS[SHARED]
    layout = tuple((bit, start, start) for bit, start in zip(bits, STARTS))
    near, far = tuple(range(group)), tuple(range(group, workers))
    pieces, spots = [], []
    *out, matrix = mix(far, here, None, (clip_radius, packed), chunks[:SHARED], layout[:SHARED], workers, half)
    for mask, value in zip(far, out):
        pieces.append(flip(value, "worker", mask))
        spots.append((mask, 0))
    out = mix(near, here, matrix, (), chunks, layout, workers, half)
    for mask, value in zip(near, out):
        pieces.append(flip(value, "worker", mask) if mask else value)
        spots.append((mask, 0))
    out = mix(near, here, matrix, (), [mirror], ((bit, split, 0),), workers, half)
    for mask, value in zip(near, out):
        pieces.append(flip(value, "worker", mask) if mask else value)
        spots.append((mask ^ group, split))
    new = place(here, pieces, tuple(spots), rows, width)
    return new[None], velocity[None]


def solution(mesh):
    placed = (
        P("worker", "tok", None),
        P("worker", "tok", None),
        P("worker", "tok", None),
        P("worker", "tok", None),
        P("worker", None),
        P(),
    )

    return jax.shard_map(
        per_device,
        mesh=mesh,
        in_specs=placed,
        out_specs=(P("worker", "tok", None), P("worker", "tok", None)),
        check_vma=False,
    )
```

```python
import functools
import math

import jax
import jax.numpy as jnp
import numpy as np
from jax import lax
from jax.experimental import pallas as pl
from jax.experimental.pallas import tpu as pltpu
from jax.sharding import PartitionSpec as P


D = 2048
KV_WIDTH = 512
ROUNDS = 2
LEARNING_RATE = 0.25
HIGH = lax.Precision.HIGHEST
LANES = 128
CHUNKS = (256, 256, 256, 256)
STARTS = tuple(sum(CHUNKS[:k]) for k in range(len(CHUNKS)))
COUNT = len(CHUNKS)
EARLY = 1
BITS = (-1, 0, 0, 0)
SHARED = 640


SMEM = pl.BlockSpec(memory_space=pltpu.SMEM)
VMEM = pl.BlockSpec(memory_space=pltpu.VMEM)


def flip(value, axis, mask):
    pairs = [(source, source ^ mask) for source in range(lax.axis_size(axis))]
    return lax.ppermute(value, axis, pairs)


def after(value, *others):
    return lax.optimization_barrier((value, *others))[0]


def neighbours(w, workers):
    return (w ^ 1, w ^ 2, (w - 4) % workers, (w + 4) % workers)


def pair_list(workers):
    return [(a, b) for a in range(workers) for b in range(a + 1, workers)]


def pair_rows(workers):
    return -(-len(pair_list(workers)) // 8) * 8


def product(left, right):
    return lax.dot_general(left, right, (((0,), (0,)), ((), ())), preferred_element_type=jnp.float32)


def blocks_of(left_ref, upstream_ref, rows, places, outs):
    for i, place in enumerate(places):
        left = left_ref[:, pl.ds(pl.multiple_of(place * rows, LANES), rows)]
        for k in range(COUNT):
            right = upstream_ref[:, STARTS[k] : STARTS[k] + CHUNKS[k]]
            outs[i * COUNT + k][...] = product(left, right)


def first_kernel(rows, cuts, at_ref, features_hbm, upstream_hbm, *rest):
    outs, (left_ref, upstream_ref, sems) = rest[: 2 * COUNT], rest[2 * COUNT :]
    at = at_ref[0]
    columns = pl.ds(pl.multiple_of(at // 2 * (2 * rows), LANES), 2 * rows)
    copies = []
    for i, cut in enumerate(cuts):
        copies.append(pltpu.make_async_copy(features_hbm.at[0, cut, columns], left_ref.at[cut], sems.at[2 * i]))
        copies.append(pltpu.make_async_copy(upstream_hbm.at[0, cut], upstream_ref.at[cut], sems.at[2 * i + 1]))
    for copy in copies:
        copy.start()
    side = at % 2
    left = pl.ds(pl.multiple_of((1 - side) * rows, LANES), rows)
    early = len(cuts) // 2
    for part in range(2):
        mine = cuts[early:] if part else cuts[:early]
        for copy in copies[2 * early * part :][: 2 * len(mine)]:
            copy.wait()
        down = slice(mine[0].start, mine[-1].stop)
        for k in range(COUNT):
            value = product(left_ref[down, left], upstream_ref[down, STARTS[k] : STARTS[k] + CHUNKS[k]])
            outs[k][...] = outs[k][...] + value if part else value
    blocks_of(left_ref, upstream_ref, rows, (side,), outs[COUNT:])


def second_kernel(rows, at_ref, features_ref, upstream_ref, *outs):
    at = at_ref[0]
    side = at % 2
    blocks_of(features_ref, upstream_ref, rows, (at + 1 - 2 * side, at), outs)


def multiply(at, features, upstream, rows, first):
    outs = [jax.ShapeDtypeStruct((rows, size), jnp.float32) for size in CHUNKS] * 2
    if not first:
        outs = pl.pallas_call(
            functools.partial(second_kernel, rows),
            in_specs=[SMEM, VMEM, VMEM],
            out_specs=[VMEM] * len(outs),
            out_shape=outs,
            compiler_params=pltpu.CompilerParams(vmem_limit_bytes=54 << 20),
            name="second",
        )(at, features[0], upstream[0])
        return list(outs[:COUNT]), list(outs[COUNT:])
    hbm = pl.BlockSpec(memory_space=pltpu.HBM)
    tokens = features.shape[1]
    step = tokens // 6 if tokens % 96 == 0 else tokens // 2
    cuts = [slice(start, start + step) for start in range(0, tokens, step)]
    outs = pl.pallas_call(
        functools.partial(first_kernel, rows, cuts),
        in_specs=[SMEM, hbm, hbm],
        out_specs=[VMEM] * len(outs),
        out_shape=outs,
        scratch_shapes=[
            pltpu.VMEM((tokens, 2 * rows), features.dtype),
            pltpu.VMEM(upstream.shape[1:], upstream.dtype),
            pltpu.SemaphoreType.DMA((2 * len(cuts),)),
        ],
        compiler_params=pltpu.CompilerParams(vmem_limit_bytes=59 << 20),
        name="first",
    )(at, features, upstream)
    return list(outs[:COUNT]), list(outs[COUNT:])


def base_kernel(weights_ref, momentum_ref, out_ref):
    out_ref[...] = weights_ref[...] - (0.5 * LEARNING_RATE) * momentum_ref[...]


def base(weights, momentum):
    return pl.pallas_call(
        base_kernel,
        in_specs=[VMEM, VMEM],
        out_specs=VMEM,
        out_shape=jax.ShapeDtypeStruct(weights.shape, jnp.float32),
        compiler_params=pltpu.CompilerParams(vmem_limit_bytes=8 << 20),
        name="base",
    )(weights, momentum)


def add_kernel(*refs):
    value = refs[0][...]
    for ref in refs[1:-1]:
        value = value + ref[...]
    refs[-1][...] = value


def add(*terms):
    return pl.pallas_call(
        add_kernel,
        in_specs=[VMEM] * len(terms),
        out_specs=VMEM,
        out_shape=jax.ShapeDtypeStruct(terms[0].shape, terms[0].dtype),
        compiler_params=pltpu.CompilerParams(vmem_limit_bytes=8 << 20),
        name="add",
    )(*terms)


def velocity_kernel(cut, gradient_ref, momentum_ref, *rest):
    out_ref, scratch_ref, sem = rest[-3:]
    scratch_ref[...] = 0.5 * momentum_ref[:, cut] + gradient_ref[...]
    copy = pltpu.make_async_copy(scratch_ref, out_ref.at[:, cut], sem)
    copy.start()
    copy.wait()


def velocity_chunk(gradient, momentum, velocity, k):
    hbm = pl.BlockSpec(memory_space=pl.ANY)
    cut = slice(STARTS[k], STARTS[k] + CHUNKS[k])
    more = () if velocity is None else (velocity,)
    return pl.pallas_call(
        functools.partial(velocity_kernel, cut),
        in_specs=[VMEM, VMEM] + [hbm] * len(more),
        out_specs=hbm,
        out_shape=jax.ShapeDtypeStruct(momentum.shape, jnp.float32),
        scratch_shapes=[pltpu.VMEM(gradient.shape, jnp.float32), pltpu.SemaphoreType.DMA],
        input_output_aliases={2: 0} if more else {},
        compiler_params=pltpu.CompilerParams(vmem_limit_bytes=8 << 20),
        name="velocity",
    )(gradient, momentum, *more)


def without(value, bit):
    return (value >> (bit + 1)) << bit | value & ((1 << bit) - 1)


def spread_bits(value, bit):
    return (value >> bit) << (bit + 1) | value & ((1 << bit) - 1)


def update_kernel(k, count, bit, me_ref, *rest):
    terms, (base_ref, gradient_ref, keep_ref, send_ref) = rest[:count], rest[count:]
    cut = slice(STARTS[k], STARTS[k] + CHUNKS[k])
    gradient = terms[0][...]
    for term in terms[1:]:
        gradient = gradient + term[...]
    gradient_ref[...] = gradient
    current = base_ref[:, cut] - LEARNING_RATE * gradient
    side = (me_ref[0] >> bit) & 1
    slots, size, _ = keep_ref.shape
    for worker in range(2 * slots):
        piece = current[worker * size : (worker + 1) * size]
        for out, mine in ((keep_ref, worker >> bit & 1), (send_ref, 1 - (worker >> bit & 1))):

            @pl.when(side == mine)
            def _(out=out, piece=piece, slot=without(worker, bit)):
                out[slot] = piece


def update(me, terms, start, k, workers, bit):
    rows = terms[0].shape[0]
    full = jax.ShapeDtypeStruct(terms[0].shape, jnp.float32)
    part = jax.ShapeDtypeStruct((workers // 2, rows // workers, CHUNKS[k]), jnp.float32)
    return pl.pallas_call(
        functools.partial(update_kernel, k, len(terms), bit),
        in_specs=[SMEM] + [VMEM] * (len(terms) + 1),
        out_specs=[VMEM] * 3,
        out_shape=[full, part, part],
        compiler_params=pltpu.CompilerParams(vmem_limit_bytes=8 << 20),
        name="update",
    )(me, *terms, start)


def regroup_kernel(bit, turn, skips, me_ref, *rest):
    group = rest[0].shape[0]
    parts, outs = rest[:-group], rest[-group:]
    rank = without(me_ref[0], bit) ^ turn
    for i, out in enumerate(outs):
        start = 0
        for place in range(0, len(parts), 2):
            skip = skips[place // 2]
            width = parts[place].shape[2] - skip
            for side in range(2):
                out[side, :, start : start + width] = parts[place + side][rank ^ i, :, skip:]
            start += width


def regroup(me, parts, bit, turn=0, skips=(0,)):
    group, rows, _ = parts[0].shape
    width = sum(part.shape[2] - skip for part, skip in zip(parts[::2], skips))
    return pl.pallas_call(
        functools.partial(regroup_kernel, bit, turn, skips),
        in_specs=[SMEM] + [VMEM] * len(parts),
        out_specs=[VMEM] * group,
        out_shape=[jax.ShapeDtypeStruct((2, rows, width), jnp.float32)] * group,
        compiler_params=pltpu.CompilerParams(vmem_limit_bytes=8 << 20),
        name="regroup",
    )(me, *parts)


def pieces_of(refs, bit, cut):
    masks = range(2 * len(refs))
    return [refs[without(mask, bit)][mask >> bit & 1, :, cut] for mask in masks]


def gap_row(left, right):
    gap = left - right
    return jnp.sum(gap * gap, axis=0, keepdims=True)


def add_squares(refs, bit, h_of, rows, sums_ref):
    for lane, h in enumerate(h_of):
        old = pieces_of(refs, bit, slice(lane * LANES, (lane + 1) * LANES))
        for place, (a, b) in enumerate(pair_list(len(old))):
            at = slice(h * rows + place, h * rows + place + 1)
            sums_ref[at, :] = sums_ref[at, :] + gap_row(old[a], old[b])


def squares_kernel(bit, h_of, *rest):
    refs, sums_ref = rest[:-1], rest[-1]
    sums_ref[...] = jnp.zeros_like(sums_ref)
    add_squares(refs, bit, h_of, sums_ref.shape[0] // 2, sums_ref)


def squares(pieces, workers, bit, h_of):
    return pl.pallas_call(
        functools.partial(squares_kernel, bit, h_of),
        in_specs=[VMEM] * len(pieces),
        out_specs=VMEM,
        out_shape=jax.ShapeDtypeStruct((2 * pair_rows(workers), LANES), jnp.float32),
        compiler_params=pltpu.CompilerParams(vmem_limit_bytes=4 << 20),
        name="squares",
    )(*pieces)


def lane_sums(sums):
    ones = jnp.ones((8, LANES), jnp.float32)
    return lax.dot_general(ones, sums, (((1,), (1,)), ((), ())), precision=HIGH, preferred_element_type=jnp.float32)


def pack_kernel(workers, tokens, parts, bit, h_of, me_ref, mix_ref, *rest):
    rows = pair_rows(workers)
    sums, refs = rest[:parts], rest[parts:-3]
    packed_ref, table_ref, total_ref = rest[-3:]
    me = me_ref[0]
    total = sums[0][...]
    for part in sums[1:]:
        total = total + part[...]
    total_ref[...] = total
    add_squares(refs, bit, h_of, rows, total_ref)
    packed_ref[...] = jnp.zeros_like(packed_ref)
    for h in range(2):
        for place, (a, b) in enumerate(pair_list(workers)):
            row = total_ref[h * rows + place : h * rows + place + 1, :]
            table_ref[a * workers + b : a * workers + b + 1, :] = row
            table_ref[b * workers + a : b * workers + a + 1, :] = row
        for place, (a, b) in enumerate(pair_list(workers)):
            row = table_ref[pl.ds((a ^ me) * workers + (b ^ me), 1), :]
            total_ref[h * rows + place : h * rows + place + 1, :] = row
        packed_ref[h : h + 1, 0:rows] = lane_sums(total_ref[h * rows : (h + 1) * rows, :])[0:1]
    lane = lax.broadcasted_iota(jnp.int32, (1, LANES), 1)
    row = jnp.zeros((1, LANES), jnp.float32)
    for k in range(5):
        weight = mix_ref[0, k].astype(jnp.float32) * (1.0 / tokens)
        row = row + jnp.where(lane == me * 5 + k, weight, 0.0)
    packed_ref[2:3, :] = row


def pack(sums, pieces, mix_weights, me, workers, tokens, bit, h_of):
    return pl.pallas_call(
        functools.partial(pack_kernel, workers, tokens, len(sums), bit, h_of),
        in_specs=[SMEM, SMEM] + [VMEM] * (len(sums) + len(pieces)),
        out_specs=VMEM,
        out_shape=jax.ShapeDtypeStruct((8, LANES), jnp.float32),
        scratch_shapes=[
            pltpu.VMEM((workers * workers, LANES), jnp.float32),
            pltpu.VMEM((2 * pair_rows(workers), LANES), jnp.float32),
        ],
        compiler_params=pltpu.CompilerParams(vmem_limit_bytes=4 << 20),
        name="pack",
    )(me, mix_weights, *sums, *pieces)


def selectors(workers):
    table = np.zeros((5, workers, workers, LANES), np.float32)
    for place, (a, b) in enumerate(pair_list(workers)):
        table[0, a, b, place] = table[0, b, a, place] = 1.0
    for w in range(workers):
        for k, j in enumerate(neighbours(w, workers)):
            table[1, w, j, w * 5 + k + 1] += 1.0
            table[3, j, w, w * 5 + k + 1] += 1.0
        table[2, w, :, w * 5 : w * 5 + 5] = 1.0
        table[4, :, w, w * 5 : w * 5 + 5] = 1.0
    return table.reshape(-1, LANES)


def spread(select, row):
    wide = jnp.broadcast_to(row, (LANES, LANES))
    return lax.dot_general(select, wide, (((1,), (1,)), ((), ())), precision=HIGH, preferred_element_type=jnp.float32)


def fill_matrices(workers, clip_ref, packed_ref, select_ref, matrix_ref):
    size = workers * workers
    table = lambda k: select_ref[k * size : (k + 1) * size, :]
    rows_of = lambda flat: [flat[w * workers : (w + 1) * workers] for w in range(workers)]
    mixing = packed_ref[2:3, :]
    share = rows_of(spread(table(1), mixing) / spread(table(2), mixing))
    share_t = rows_of(spread(table(3), mixing) / spread(table(4), mixing))
    place = lax.broadcasted_iota(jnp.int32, (workers, LANES), 0)
    eye = [jnp.where(place == w, 1.0, 0.0) for w in range(workers)]
    radius = [clip_ref[r].astype(jnp.float32) * (math.sqrt(D * KV_WIDTH) / 1000.0) for r in range(ROUNDS)]

    def times(left, right):
        out = []
        for w in range(workers):
            total = None
            for j in range(workers):
                term = left[w][j : j + 1, :] * right[j]
                total = term if total is None else total + term
            out.append(total)
        return out

    for h in range(2):
        first = rows_of(spread(table(0), packed_ref[h : h + 1, :]))
        now, total, total_t = first, None, None
        for r in range(ROUNDS):
            factor = [radius[r] / jnp.maximum(jnp.sqrt(d), radius[r]) for d in now]
            step = [s * f for s, f in zip(share, factor)]
            step = [a + e * (1.0 - jnp.sum(a, axis=0, keepdims=True)) for a, e in zip(step, eye)]
            total = step if total is None else times(step, total)
            if r + 1 < ROUNDS:
                step_t = [s * f for s, f in zip(share_t, factor)]
                keep = 1.0 - functools.reduce(lambda a, b: a + b, step_t)
                step_t = [a + e * keep for a, e in zip(step_t, eye)]
                total_t = step_t if total_t is None else times(total_t, step_t)
                inner = times(times(total, first), total_t)
                diag = functools.reduce(lambda a, b: a + b, [i * e for i, e in zip(inner, eye)])
                now = [
                    jnp.maximum(i - 0.5 * (diag + diag[w : w + 1, :]), 0.0) for w, i in enumerate(inner)
                ]
        for w in range(workers):
            at = h * size + w * workers
            matrix_ref[at : at + workers, :] = total[w]


def mix_kernel(workers, half, layout, masks, first, me_ref, *rest):
    if first:
        clip_ref, packed_ref, select_ref, *rest = rest
        matrix_ref, *rest = rest[-1:] + rest[:-1]
        fill_matrices(workers, clip_ref, packed_ref, select_ref, matrix_ref)
    else:
        matrix_ref, *rest = rest
    me = me_ref[0]
    for bit, start, into, size in layout:
        refs, rest = rest[: workers // 2], rest[workers // 2 :]
        for lane in range(0, size, LANES):
            base = (start + lane) // half * workers * workers
            old = pieces_of(refs, bit, slice(lane, lane + LANES))
            for mask, out in zip(masks, rest[-len(masks) :]):
                value = None
                for other, rows in enumerate(old):
                    share = matrix_ref[pl.ds(base + (me ^ mask) * workers + (me ^ other), 1), :]
                    value = share * rows if value is None else value + share * rows
                out[:, into + lane : into + lane + LANES] = value


def mix(masks, me, matrix, head, chunks, layout, workers, half):
    first = matrix is None
    rows = chunks[0][0].shape[1]
    width = sum(size for _, _, _, size in layout)
    table = jax.ShapeDtypeStruct((2 * workers * workers, LANES), jnp.float32)
    head = (*head, selectors(workers)) if first else (matrix,)
    return pl.pallas_call(
        functools.partial(mix_kernel, workers, half, layout, masks, first),
        in_specs=[SMEM] * (1 + first) + [VMEM] * (len(head) - first + sum(len(chunk) for chunk in chunks)),
        out_specs=[VMEM] * (len(masks) + first),
        out_shape=[jax.ShapeDtypeStruct((rows, width), jnp.float32)] * len(masks) + [table] * first,
        compiler_params=pltpu.CompilerParams(vmem_limit_bytes=16 << 20),
        name="mix",
    )(me, *head, *[piece for chunk in chunks for piece in chunk])


def place_kernel(spots, me_ref, *rest):
    pieces, out_ref, sems = rest[:-2], rest[-2], rest[-1]
    copies = []
    for i, (mask, start) in enumerate(spots):
        rows, width = pieces[i].shape
        at = pl.ds(pl.multiple_of((me_ref[0] ^ mask) * rows, 8), rows)
        copies.append(pltpu.make_async_copy(pieces[i], out_ref.at[at, start : start + width], sems.at[i]))
        copies[i].start()
    for copy in copies:
        copy.wait()


def place(me, pieces, spots, rows, width):
    return pl.pallas_call(
        functools.partial(place_kernel, spots),
        in_specs=[SMEM] + [pl.BlockSpec(memory_space=pl.ANY)] * len(pieces),
        out_specs=pl.BlockSpec(memory_space=pl.ANY),
        out_shape=jax.ShapeDtypeStruct((rows, width), jnp.float32),
        scratch_shapes=[pltpu.SemaphoreType.DMA((len(pieces),))],
        compiler_params=pltpu.CompilerParams(vmem_limit_bytes=4 << 20),
        name="place",
    )(me, *pieces)


def per_device(inputs, cotangent, weights, momentum, mix_weights, clip_radius):
    tokens = lax.axis_size("tok")
    workers = lax.axis_size("worker")
    group = workers // 2
    tok, me = lax.axis_index("tok"), lax.axis_index("worker")
    here = me.reshape(1)
    rows, width = weights.shape[1:]
    half = width // 2
    h_of = [tuple((start + lane) // half for lane in range(0, size, LANES)) for start, size in zip(STARTS, CHUNKS)]
    levels = tokens.bit_length() - 1
    order = [None]

    last = 1 << (levels - 1)
    index = lambda offset: (tok ^ offset).reshape(1)
    leaves = {}
    for offset in [*range(last, tokens, 2), *range(0, last, 2)]:
        at = index(offset) if order[0] is None else after(index(offset), order[0])
        leaves[offset + 1], leaves[offset] = multiply(at, inputs, cotangent, rows, True)
        order[0] = leaves[offset][0]

    def arrived(offset, level, k):
        terms = []
        for step in range(1, level + 1):
            mask = 1 << (step - 1)
            away = reduced(offset ^ mask, step - 1, k)
            terms.append(flip(away, "tok", mask))
        return terms

    def reduced(offset, level, k):
        return add(leaves[offset][k], *arrived(offset, level, k)) if level else leaves[offset][k]

    def send_terms(k, *gates):
        leaves[last][k] = after(leaves[last][k], *gates)
        away = reduced(last, levels - 1, k)
        return flip(away, "tok", last), away

    aways, away = [], leaves[last][0]
    for k in range(EARLY):
        moved, away = send_terms(k, away)
        aways.append(moved)
    extras = [arrived(0, levels - 1, k) for k in range(COUNT)]
    moved, away = send_terms(1, away, leaves[0][0])
    aways.append(moved)
    start = base(weights[0], momentum[0])
    velocity, chunks, sums = None, [], []
    bits = [bit % (workers.bit_length() - 1) for bit in BITS]
    held, skips = [], ()
    for k in range(COUNT):
        away = after(aways[k], gradient) if k else aways[k]
        terms = [leaves[0][k], *extras[k], away]
        gradient, keep, send = update(here, terms, start, k, workers, bits[k])
        got = flip(send, "worker", 1 << bits[k])
        pieces = list(regroup(here, (keep, got), bits[k]))
        if STARTS[k] + CHUNKS[k] > SHARED:
            held += [keep, got]
            skips += (max(SHARED - STARTS[k], 0),)
        for i in reversed(range(1, group)):
            pieces[i] = flip(pieces[i], "worker", spread_bits(i, bits[k]))
        chunks.append(pieces)
        if k < COUNT - 1:
            sums.append(squares(pieces, workers, bits[k], h_of[k]))
        if k == 0:
            moved, _ = send_terms(len(aways), gradient)
            aways.append(moved)
        velocity = velocity_chunk(gradient, momentum[0], velocity, k)
        if 0 < k and len(aways) < COUNT:
            moved, _ = send_terms(len(aways), velocity)
            aways.append(moved)
    packed = pack(sums, chunks[-1], mix_weights, here, workers, tokens, bits[-1], h_of[-1])
    bit = bits[-1]
    mirror = list(regroup(here, held, bit, without(group, bit), skips))
    later = [*range(group // 2, group), *range(1, group // 2)]
    rounds = [("worker", [2 * i for i in range(1, group)]), ("worker", [1])]
    rounds += [("tok", [1 << level]) for level in range(levels)]
    for axis, masks in rounds:
        packed = sum([flip(packed, axis, mask) for mask in masks], packed)
        if later:
            i = later.pop(0)
            mirror[i] = flip(after(mirror[i], packed), "worker", spread_bits(i, bit))
    for i in later:
        mirror[i] = flip(mirror[i], "worker", spread_bits(i, bit))
    layout = tuple((bit, start, start, size) for bit, start, size in zip(bits, STARTS, CHUNKS))
    apart = tuple((bit, start, start, min(size, SHARED - start)) for bit, start, _, size in layout if start < SHARED)
    near, far = tuple(range(group)), tuple(range(group, workers))
    pieces, spots = [], []
    *out, matrix = mix(near, here, None, (clip_radius, packed), chunks, layout, workers, half)
    for mask, value in zip(near, out):
        pieces.append(flip(value, "worker", mask) if mask else value)
        spots.append((mask, 0))
    out = mix(far, here, matrix, (), chunks[: len(apart)], apart, workers, half)
    for mask, value in zip(far, out):
        pieces.append(flip(value, "worker", mask))
        spots.append((mask, 0))
    out = mix(near, here, matrix, (), [mirror], ((bit, SHARED, 0, width - SHARED),), workers, half)
    for mask, value in zip(near, out):
        pieces.append(flip(value, "worker", mask) if mask else value)
        spots.append((mask ^ group, SHARED))
    new = place(here, pieces, tuple(spots), rows, width)
    return new[None], velocity[None]


def solution(mesh):
    placed = (
        P("worker", "tok", None),
        P("worker", "tok", None),
        P("worker", "tok", None),
        P("worker", "tok", None),
        P("worker", None),
        P(),
    )

    return jax.shard_map(
        per_device,
        mesh=mesh,
        in_specs=placed,
        out_specs=(P("worker", "tok", None), P("worker", "tok", None)),
        check_vma=False,
    )
```

```python
import functools
import math

import jax
import jax.numpy as jnp
import numpy as np
from jax import lax
from jax.experimental import pallas as pl
from jax.experimental.pallas import tpu as pltpu
from jax.sharding import PartitionSpec as P


D = 2048
KV_WIDTH = 512
ROUNDS = 2
LEARNING_RATE = 0.25
HIGH = lax.Precision.HIGHEST
LANES = 128
CHUNKS = (256, 256, 256, 256)
STARTS = tuple(sum(CHUNKS[:k]) for k in range(len(CHUNKS)))
COUNT = len(CHUNKS)
EARLY = 1
BITS = (-1, 0, 0, 0)
SHARED = 640


SMEM = pl.BlockSpec(memory_space=pltpu.SMEM)
VMEM = pl.BlockSpec(memory_space=pltpu.VMEM)


def flip(value, axis, mask):
    pairs = [(source, source ^ mask) for source in range(lax.axis_size(axis))]
    return lax.ppermute(value, axis, pairs)


def after(value, *others):
    return lax.optimization_barrier((value, *others))[0]


def neighbours(w, workers):
    return (w ^ 1, w ^ 2, (w - 4) % workers, (w + 4) % workers)


def pair_list(workers):
    return [(a, b) for a in range(workers) for b in range(a + 1, workers)]


def pair_rows(workers):
    return -(-len(pair_list(workers)) // 8) * 8


def product(left, right):
    return lax.dot_general(left, right, (((0,), (0,)), ((), ())), preferred_element_type=jnp.float32)


def blocks_of(left_ref, upstream_ref, rows, places, outs):
    for i, place in enumerate(places):
        left = left_ref[:, pl.ds(pl.multiple_of(place * rows, LANES), rows)]
        for k in range(COUNT):
            right = upstream_ref[:, STARTS[k] : STARTS[k] + CHUNKS[k]]
            outs[i * COUNT + k][...] = product(left, right)


def first_kernel(rows, cuts, at_ref, features_hbm, upstream_hbm, *rest):
    outs, (left_ref, upstream_ref, sems) = rest[: 2 * COUNT], rest[2 * COUNT :]
    at = at_ref[0]
    columns = pl.ds(pl.multiple_of(at // 2 * (2 * rows), LANES), 2 * rows)
    copies = []
    for i, cut in enumerate(cuts):
        copies.append(pltpu.make_async_copy(features_hbm.at[0, cut, columns], left_ref.at[cut], sems.at[2 * i]))
        copies.append(pltpu.make_async_copy(upstream_hbm.at[0, cut], upstream_ref.at[cut], sems.at[2 * i + 1]))
    for copy in copies:
        copy.start()
    side = at % 2
    left = pl.ds(pl.multiple_of((1 - side) * rows, LANES), rows)
    early = len(cuts) // 2
    for part in range(2):
        mine = cuts[early:] if part else cuts[:early]
        for copy in copies[2 * early * part :][: 2 * len(mine)]:
            copy.wait()
        down = slice(mine[0].start, mine[-1].stop)
        for k in range(COUNT):
            value = product(left_ref[down, left], upstream_ref[down, STARTS[k] : STARTS[k] + CHUNKS[k]])
            outs[k][...] = outs[k][...] + value if part else value
    blocks_of(left_ref, upstream_ref, rows, (side,), outs[COUNT:])


def second_kernel(rows, at_ref, features_ref, upstream_ref, *outs):
    at = at_ref[0]
    side = at % 2
    blocks_of(features_ref, upstream_ref, rows, (at + 1 - 2 * side, at), outs)


def multiply(at, features, upstream, rows, first):
    outs = [jax.ShapeDtypeStruct((rows, size), jnp.float32) for size in CHUNKS] * 2
    if not first:
        outs = pl.pallas_call(
            functools.partial(second_kernel, rows),
            in_specs=[SMEM, VMEM, VMEM],
            out_specs=[VMEM] * len(outs),
            out_shape=outs,
            compiler_params=pltpu.CompilerParams(vmem_limit_bytes=54 << 20),
            name="second",
        )(at, features[0], upstream[0])
        return list(outs[:COUNT]), list(outs[COUNT:])
    hbm = pl.BlockSpec(memory_space=pltpu.HBM)
    tokens = features.shape[1]
    step = tokens // 6 if tokens % 96 == 0 else tokens // 2
    cuts = [slice(start, start + step) for start in range(0, tokens, step)]
    outs = pl.pallas_call(
        functools.partial(first_kernel, rows, cuts),
        in_specs=[SMEM, hbm, hbm],
        out_specs=[VMEM] * len(outs),
        out_shape=outs,
        scratch_shapes=[
            pltpu.VMEM((tokens, 2 * rows), features.dtype),
            pltpu.VMEM(upstream.shape[1:], upstream.dtype),
            pltpu.SemaphoreType.DMA((2 * len(cuts),)),
        ],
        compiler_params=pltpu.CompilerParams(vmem_limit_bytes=59 << 20),
        name="first",
    )(at, features, upstream)
    return list(outs[:COUNT]), list(outs[COUNT:])


def tick_kernel(in_ref, out_ref):
    out_ref[...] = in_ref[...]


def tick(value):
    return pl.pallas_call(
        tick_kernel,
        in_specs=[VMEM],
        out_specs=VMEM,
        out_shape=jax.ShapeDtypeStruct(value.shape, value.dtype),
        compiler_params=pltpu.CompilerParams(vmem_limit_bytes=4 << 20),
        name="tick",
    )(value)


def base_kernel(weights_ref, momentum_ref, out_ref):
    out_ref[...] = weights_ref[...] - (0.5 * LEARNING_RATE) * momentum_ref[...]


def base(weights, momentum):
    return pl.pallas_call(
        base_kernel,
        in_specs=[VMEM, VMEM],
        out_specs=VMEM,
        out_shape=jax.ShapeDtypeStruct(weights.shape, jnp.float32),
        compiler_params=pltpu.CompilerParams(vmem_limit_bytes=8 << 20),
        name="base",
    )(weights, momentum)


def add_kernel(*refs):
    value = refs[0][...]
    for ref in refs[1:-1]:
        value = value + ref[...]
    refs[-1][...] = value


def add(*terms):
    return pl.pallas_call(
        add_kernel,
        in_specs=[VMEM] * len(terms),
        out_specs=VMEM,
        out_shape=jax.ShapeDtypeStruct(terms[0].shape, terms[0].dtype),
        compiler_params=pltpu.CompilerParams(vmem_limit_bytes=8 << 20),
        name="add",
    )(*terms)


def velocity_kernel(cut, gradient_ref, momentum_ref, *rest):
    out_ref, scratch_ref, sem = rest[-3:]
    scratch_ref[...] = 0.5 * momentum_ref[:, cut] + gradient_ref[...]
    copy = pltpu.make_async_copy(scratch_ref, out_ref.at[:, cut], sem)
    copy.start()
    copy.wait()


def velocity_chunk(gradient, momentum, velocity, k):
    hbm = pl.BlockSpec(memory_space=pl.ANY)
    cut = slice(STARTS[k], STARTS[k] + CHUNKS[k])
    more = () if velocity is None else (velocity,)
    return pl.pallas_call(
        functools.partial(velocity_kernel, cut),
        in_specs=[VMEM, VMEM] + [hbm] * len(more),
        out_specs=hbm,
        out_shape=jax.ShapeDtypeStruct(momentum.shape, jnp.float32),
        scratch_shapes=[pltpu.VMEM(gradient.shape, jnp.float32), pltpu.SemaphoreType.DMA],
        input_output_aliases={2: 0} if more else {},
        compiler_params=pltpu.CompilerParams(vmem_limit_bytes=8 << 20),
        name="velocity",
    )(gradient, momentum, *more)


def without(value, bit):
    return (value >> (bit + 1)) << bit | value & ((1 << bit) - 1)


def spread_bits(value, bit):
    return (value >> bit) << (bit + 1) | value & ((1 << bit) - 1)


def update_kernel(k, count, bit, me_ref, *rest):
    terms, (base_ref, gradient_ref, keep_ref, send_ref) = rest[:count], rest[count:]
    cut = slice(STARTS[k], STARTS[k] + CHUNKS[k])
    gradient = terms[0][...]
    for term in terms[1:]:
        gradient = gradient + term[...]
    gradient_ref[...] = gradient
    current = base_ref[:, cut] - LEARNING_RATE * gradient
    side = (me_ref[0] >> bit) & 1
    slots, size, _ = keep_ref.shape
    for worker in range(2 * slots):
        piece = current[worker * size : (worker + 1) * size]
        for out, mine in ((keep_ref, worker >> bit & 1), (send_ref, 1 - (worker >> bit & 1))):

            @pl.when(side == mine)
            def _(out=out, piece=piece, slot=without(worker, bit)):
                out[slot] = piece


def update(me, terms, start, k, workers, bit):
    rows = terms[0].shape[0]
    full = jax.ShapeDtypeStruct(terms[0].shape, jnp.float32)
    part = jax.ShapeDtypeStruct((workers // 2, rows // workers, CHUNKS[k]), jnp.float32)
    return pl.pallas_call(
        functools.partial(update_kernel, k, len(terms), bit),
        in_specs=[SMEM] + [VMEM] * (len(terms) + 1),
        out_specs=[VMEM] * 3,
        out_shape=[full, part, part],
        compiler_params=pltpu.CompilerParams(vmem_limit_bytes=8 << 20),
        name="update",
    )(me, *terms, start)


def regroup_kernel(bit, turn, skips, me_ref, *rest):
    group = rest[0].shape[0]
    parts, outs = rest[:-group], rest[-group:]
    rank = without(me_ref[0], bit) ^ turn
    for i, out in enumerate(outs):
        start = 0
        for place in range(0, len(parts), 2):
            skip = skips[place // 2]
            width = parts[place].shape[2] - skip
            for side in range(2):
                out[side, :, start : start + width] = parts[place + side][rank ^ i, :, skip:]
            start += width


def regroup(me, parts, bit, turn=0, skips=(0,)):
    group, rows, _ = parts[0].shape
    width = sum(part.shape[2] - skip for part, skip in zip(parts[::2], skips))
    return pl.pallas_call(
        functools.partial(regroup_kernel, bit, turn, skips),
        in_specs=[SMEM] + [VMEM] * len(parts),
        out_specs=[VMEM] * group,
        out_shape=[jax.ShapeDtypeStruct((2, rows, width), jnp.float32)] * group,
        compiler_params=pltpu.CompilerParams(vmem_limit_bytes=8 << 20),
        name="regroup",
    )(me, *parts)


def pieces_of(refs, bit, cut):
    masks = range(2 * len(refs))
    return [refs[without(mask, bit)][mask >> bit & 1, :, cut] for mask in masks]


def gap_row(left, right):
    gap = left - right
    return jnp.sum(gap * gap, axis=0, keepdims=True)


def add_squares(refs, bit, h_of, rows, sums_ref):
    for lane, h in enumerate(h_of):
        old = pieces_of(refs, bit, slice(lane * LANES, (lane + 1) * LANES))
        for place, (a, b) in enumerate(pair_list(len(old))):
            at = slice(h * rows + place, h * rows + place + 1)
            sums_ref[at, :] = sums_ref[at, :] + gap_row(old[a], old[b])


def squares_kernel(bit, h_of, *rest):
    refs, sums_ref = rest[:-1], rest[-1]
    sums_ref[...] = jnp.zeros_like(sums_ref)
    add_squares(refs, bit, h_of, sums_ref.shape[0] // 2, sums_ref)


def squares(pieces, workers, bit, h_of):
    return pl.pallas_call(
        functools.partial(squares_kernel, bit, h_of),
        in_specs=[VMEM] * len(pieces),
        out_specs=VMEM,
        out_shape=jax.ShapeDtypeStruct((2 * pair_rows(workers), LANES), jnp.float32),
        compiler_params=pltpu.CompilerParams(vmem_limit_bytes=4 << 20),
        name="squares",
    )(*pieces)


def lane_sums(sums):
    ones = jnp.ones((8, LANES), jnp.float32)
    return lax.dot_general(ones, sums, (((1,), (1,)), ((), ())), precision=HIGH, preferred_element_type=jnp.float32)


def pack_kernel(workers, tokens, parts, bit, h_of, me_ref, mix_ref, *rest):
    rows = pair_rows(workers)
    sums, refs = rest[:parts], rest[parts:-3]
    packed_ref, table_ref, total_ref = rest[-3:]
    me = me_ref[0]
    total = sums[0][...]
    for part in sums[1:]:
        total = total + part[...]
    total_ref[...] = total
    add_squares(refs, bit, h_of, rows, total_ref)
    packed_ref[...] = jnp.zeros_like(packed_ref)
    for h in range(2):
        for place, (a, b) in enumerate(pair_list(workers)):
            row = total_ref[h * rows + place : h * rows + place + 1, :]
            table_ref[a * workers + b : a * workers + b + 1, :] = row
            table_ref[b * workers + a : b * workers + a + 1, :] = row
        for place, (a, b) in enumerate(pair_list(workers)):
            row = table_ref[pl.ds((a ^ me) * workers + (b ^ me), 1), :]
            total_ref[h * rows + place : h * rows + place + 1, :] = row
        packed_ref[h : h + 1, 0:rows] = lane_sums(total_ref[h * rows : (h + 1) * rows, :])[0:1]
    lane = lax.broadcasted_iota(jnp.int32, (1, LANES), 1)
    row = jnp.zeros((1, LANES), jnp.float32)
    for k in range(5):
        weight = mix_ref[0, k].astype(jnp.float32) * (1.0 / tokens)
        row = row + jnp.where(lane == me * 5 + k, weight, 0.0)
    packed_ref[2:3, :] = row


def pack(sums, pieces, mix_weights, me, workers, tokens, bit, h_of):
    return pl.pallas_call(
        functools.partial(pack_kernel, workers, tokens, len(sums), bit, h_of),
        in_specs=[SMEM, SMEM] + [VMEM] * (len(sums) + len(pieces)),
        out_specs=VMEM,
        out_shape=jax.ShapeDtypeStruct((8, LANES), jnp.float32),
        scratch_shapes=[
            pltpu.VMEM((workers * workers, LANES), jnp.float32),
            pltpu.VMEM((2 * pair_rows(workers), LANES), jnp.float32),
        ],
        compiler_params=pltpu.CompilerParams(vmem_limit_bytes=4 << 20),
        name="pack",
    )(me, mix_weights, *sums, *pieces)


def selectors(workers):
    table = np.zeros((5, workers, workers, LANES), np.float32)
    for place, (a, b) in enumerate(pair_list(workers)):
        table[0, a, b, place] = table[0, b, a, place] = 1.0
    for w in range(workers):
        for k, j in enumerate(neighbours(w, workers)):
            table[1, w, j, w * 5 + k + 1] += 1.0
            table[3, j, w, w * 5 + k + 1] += 1.0
        table[2, w, :, w * 5 : w * 5 + 5] = 1.0
        table[4, :, w, w * 5 : w * 5 + 5] = 1.0
    return table.reshape(-1, LANES)


def spread(select, row):
    wide = jnp.broadcast_to(row, (LANES, LANES))
    return lax.dot_general(select, wide, (((1,), (1,)), ((), ())), precision=HIGH, preferred_element_type=jnp.float32)


def fill_matrices(workers, clip_ref, packed_ref, select_ref, matrix_ref):
    size = workers * workers
    table = lambda k: select_ref[k * size : (k + 1) * size, :]
    rows_of = lambda flat: [flat[w * workers : (w + 1) * workers] for w in range(workers)]
    mixing = packed_ref[2:3, :]
    share = rows_of(spread(table(1), mixing) / spread(table(2), mixing))
    share_t = rows_of(spread(table(3), mixing) / spread(table(4), mixing))
    place = lax.broadcasted_iota(jnp.int32, (workers, LANES), 0)
    eye = [jnp.where(place == w, 1.0, 0.0) for w in range(workers)]
    radius = [clip_ref[r].astype(jnp.float32) * (math.sqrt(D * KV_WIDTH) / 1000.0) for r in range(ROUNDS)]

    def times(left, right):
        out = []
        for w in range(workers):
            total = None
            for j in range(workers):
                term = left[w][j : j + 1, :] * right[j]
                total = term if total is None else total + term
            out.append(total)
        return out

    for h in range(2):
        first = rows_of(spread(table(0), packed_ref[h : h + 1, :]))
        now, total, total_t = first, None, None
        for r in range(ROUNDS):
            factor = [radius[r] / jnp.maximum(jnp.sqrt(d), radius[r]) for d in now]
            step = [s * f for s, f in zip(share, factor)]
            step = [a + e * (1.0 - jnp.sum(a, axis=0, keepdims=True)) for a, e in zip(step, eye)]
            total = step if total is None else times(step, total)
            if r + 1 < ROUNDS:
                step_t = [s * f for s, f in zip(share_t, factor)]
                keep = 1.0 - functools.reduce(lambda a, b: a + b, step_t)
                step_t = [a + e * keep for a, e in zip(step_t, eye)]
                total_t = step_t if total_t is None else times(total_t, step_t)
                inner = times(times(total, first), total_t)
                diag = functools.reduce(lambda a, b: a + b, [i * e for i, e in zip(inner, eye)])
                now = [
                    jnp.maximum(i - 0.5 * (diag + diag[w : w + 1, :]), 0.0) for w, i in enumerate(inner)
                ]
        for w in range(workers):
            at = h * size + w * workers
            matrix_ref[at : at + workers, :] = total[w]


def mix_kernel(workers, half, layout, masks, first, me_ref, *rest):
    if first:
        clip_ref, packed_ref, select_ref, *rest = rest
        matrix_ref, *rest = rest[-1:] + rest[:-1]
        fill_matrices(workers, clip_ref, packed_ref, select_ref, matrix_ref)
    else:
        matrix_ref, *rest = rest
    me = me_ref[0]
    for bit, start, into, size in layout:
        refs, rest = rest[: workers // 2], rest[workers // 2 :]
        for lane in range(0, size, LANES):
            base = (start + lane) // half * workers * workers
            old = pieces_of(refs, bit, slice(lane, lane + LANES))
            for mask, out in zip(masks, rest[-len(masks) :]):
                value = None
                for other, rows in enumerate(old):
                    share = matrix_ref[pl.ds(base + (me ^ mask) * workers + (me ^ other), 1), :]
                    value = share * rows if value is None else value + share * rows
                out[:, into + lane : into + lane + LANES] = value


def mix(masks, me, matrix, head, chunks, layout, workers, half):
    first = matrix is None
    rows = chunks[0][0].shape[1]
    width = sum(size for _, _, _, size in layout)
    table = jax.ShapeDtypeStruct((2 * workers * workers, LANES), jnp.float32)
    head = (*head, selectors(workers)) if first else (matrix,)
    return pl.pallas_call(
        functools.partial(mix_kernel, workers, half, layout, masks, first),
        in_specs=[SMEM] * (1 + first) + [VMEM] * (len(head) - first + sum(len(chunk) for chunk in chunks)),
        out_specs=[VMEM] * (len(masks) + first),
        out_shape=[jax.ShapeDtypeStruct((rows, width), jnp.float32)] * len(masks) + [table] * first,
        compiler_params=pltpu.CompilerParams(vmem_limit_bytes=16 << 20),
        name="mix",
    )(me, *head, *[piece for chunk in chunks for piece in chunk])


def place_kernel(spots, me_ref, *rest):
    pieces, out_ref, sems = rest[:-2], rest[-2], rest[-1]
    copies = []
    for i, (mask, start) in enumerate(spots):
        rows, width = pieces[i].shape
        at = pl.ds(pl.multiple_of((me_ref[0] ^ mask) * rows, 8), rows)
        copies.append(pltpu.make_async_copy(pieces[i], out_ref.at[at, start : start + width], sems.at[i]))
        copies[i].start()
    for copy in copies:
        copy.wait()


def place(me, pieces, spots, rows, width):
    return pl.pallas_call(
        functools.partial(place_kernel, spots),
        in_specs=[SMEM] + [pl.BlockSpec(memory_space=pl.ANY)] * len(pieces),
        out_specs=pl.BlockSpec(memory_space=pl.ANY),
        out_shape=jax.ShapeDtypeStruct((rows, width), jnp.float32),
        scratch_shapes=[pltpu.SemaphoreType.DMA((len(pieces),))],
        compiler_params=pltpu.CompilerParams(vmem_limit_bytes=4 << 20),
        name="place",
    )(me, *pieces)


def per_device(inputs, cotangent, weights, momentum, mix_weights, clip_radius):
    tokens = lax.axis_size("tok")
    workers = lax.axis_size("worker")
    group = workers // 2
    tok, me = lax.axis_index("tok"), lax.axis_index("worker")
    here = me.reshape(1)
    rows, width = weights.shape[1:]
    half = width // 2
    h_of = [tuple((start + lane) // half for lane in range(0, size, LANES)) for start, size in zip(STARTS, CHUNKS)]
    levels = tokens.bit_length() - 1
    order = [None]

    last = 1 << (levels - 1)
    index = lambda offset: (tok ^ offset).reshape(1)
    leaves = {}
    for offset in [*range(last, tokens, 2), *range(0, last, 2)]:
        at = index(offset) if order[0] is None else after(index(offset), order[0])
        leaves[offset + 1], leaves[offset] = multiply(at, inputs, cotangent, rows, True)
        order[0] = leaves[offset][0]

    def arrived(offset, level, k):
        terms = []
        for step in range(1, level + 1):
            mask = 1 << (step - 1)
            away = reduced(offset ^ mask, step - 1, k)
            terms.append(flip(away, "tok", mask))
        return terms

    def reduced(offset, level, k):
        return add(leaves[offset][k], *arrived(offset, level, k)) if level else leaves[offset][k]

    def send_terms(k, *gates):
        leaves[last][k] = after(leaves[last][k], *gates)
        away = reduced(last, levels - 1, k)
        return flip(away, "tok", last), away

    aways, away = [], leaves[last][0]
    for k in range(EARLY):
        moved, away = send_terms(k, away)
        aways.append(moved)
    extras = [arrived(0, levels - 1, k) for k in range(COUNT)]
    moved, away = send_terms(1, away, leaves[0][0])
    aways.append(moved)
    start = base(weights[0], momentum[0])
    velocity, chunks, sums = None, [], []
    bits = [bit % (workers.bit_length() - 1) for bit in BITS]
    held, skips = [], ()
    for k in range(COUNT):
        away = after(aways[k], gradient) if k else aways[k]
        terms = [leaves[0][k], *extras[k], away]
        gradient, keep, send = update(here, terms, start, k, workers, bits[k])
        got = flip(send, "worker", 1 << bits[k])
        pieces = list(regroup(here, (keep, got), bits[k]))
        if STARTS[k] + CHUNKS[k] > SHARED:
            held += [keep, got]
            skips += (max(SHARED - STARTS[k], 0),)
        for i in reversed(range(1, group)):
            pieces[i] = flip(pieces[i], "worker", spread_bits(i, bits[k]))
        chunks.append(pieces)
        if k < COUNT - 1:
            sums.append(squares(pieces, workers, bits[k], h_of[k]))
        if k == 0:
            moved, _ = send_terms(len(aways), gradient)
            aways.append(moved)
        velocity = velocity_chunk(gradient, momentum[0], velocity, k)
        if 0 < k and len(aways) < COUNT:
            moved, _ = send_terms(len(aways), velocity)
            aways.append(moved)
    packed = pack(sums, chunks[-1], mix_weights, here, workers, tokens, bits[-1], h_of[-1])
    bit = bits[-1]
    mirror = list(regroup(here, held, bit, without(group, bit), skips))
    later = [*range(group // 2, group), *range(1, group // 2)]
    i = later.pop(0)
    mirror[i] = flip(after(mirror[i], packed), "worker", spread_bits(i, bit))
    mark = tick(packed)
    rounds = [("worker", [2 * i for i in range(1, group)]), ("worker", [1])]
    rounds += [("tok", [1 << level]) for level in range(levels)]
    for axis, masks in rounds:
        terms = [packed]
        for mask in masks:
            terms.append(flip(packed, axis, mask))
        packed = sum(terms[1:], terms[0])
        if later:
            i = later.pop(0)
            mirror[i] = flip(after(mirror[i], packed), "worker", spread_bits(i, bit))
    for i in later:
        mirror[i] = flip(mirror[i], "worker", spread_bits(i, bit))
    layout = tuple((bit, start, start, size) for bit, start, size in zip(bits, STARTS, CHUNKS))
    apart = tuple((bit, start, start, min(size, SHARED - start)) for bit, start, _, size in layout if start < SHARED)
    near, far = tuple(range(group)), tuple(range(group, workers))
    pieces, spots = [], []
    *out, matrix = mix(near, here, None, (clip_radius, packed), chunks, layout, workers, half)
    for mask, value in zip(near, out):
        pieces.append(flip(value, "worker", mask) if mask else value)
        spots.append((mask, 0))
    out = mix(far, here, matrix, (), chunks[: len(apart)], apart, workers, half)
    for mask, value in zip(far, out):
        pieces.append(flip(value, "worker", mask))
        spots.append((mask, 0))
    out = mix(near, here, matrix, (), [mirror], ((bit, SHARED, 0, width - SHARED),), workers, half)
    for mask, value in zip(near, out):
        pieces.append(flip(value, "worker", mask) if mask else value)
        spots.append((mask ^ group, SHARED))
    new = place(here, [*pieces, mark], tuple(spots), rows, width)
    return new[None], velocity[None]


def solution(mesh):
    placed = (
        P("worker", "tok", None),
        P("worker", "tok", None),
        P("worker", "tok", None),
        P("worker", "tok", None),
        P("worker", None),
        P(),
    )

    return jax.shard_map(
        per_device,
        mesh=mesh,
        in_specs=placed,
        out_specs=(P("worker", "tok", None), P("worker", "tok", None)),
        check_vma=False,
    )
```
